256 devices in a mesh: ctx: 8 (over z_lo, core), ep: 32 (over y, x, z_hi).
Axes of the slice: x: 4, y: 4, z: 8 (z_hi: 2, z_lo: 4; z = z_hi * 4 + z_lo), core: 2. Of those that a mesh axis runs over, the one named last changes fastest.
Arguments:
- queries: bfloat16 [32768, 2048], P(('ctx', 'ep')), may hold values from -40 to 40
- keys: bfloat16 [32768, 256], P(('ctx', 'ep')), may hold values from -40 to 40
- values: bfloat16 [32768, 256], P(('ctx', 'ep')), may hold values from -6 to 6
- prior_out: bfloat16 [32768, 2048], P(('ctx', 'ep')), may hold values from -6 to 6
- prior_lse: float32 [32768, 16], P(('ctx', 'ep')), may hold values from 4 to 8
- residual: bfloat16 [32768, 2048], P(('ctx', 'ep')), may hold values from -40 to 40
- out_proj: bfloat16 [2048, 2048], P(('ctx', 'ep')), may hold values from -0.5 to 0.5
- norm_gain: float32 [2048], replicated, may hold values from 0.5 to 1.5
- expert_in: bfloat16 [32, 2048, 1536], P('ep'), may hold values from -0.125 to 0.125
- expert_out: bfloat16 [32, 768, 2048], P('ep'), may hold values from -0.21875 to 0.21875
- expert_ids: int32 [32768, 8], P(('ctx', 'ep')), may hold values from 0 to 31, as said below
- route_weight: float32 [32768, 8], P(('ctx', 'ep')), may hold values from 0.05 to 0.6
Outputs:
- layer_out: bfloat16 [32768, 2048], P(('ctx', 'ep'))
- attended: bfloat16 [32768, 2048], P(('ctx', 'ep'))
The draws below stay inside these ranges and needn't reach their ends.
Inputs may be any that keep to these rules, and one draw needn't show every extreme that they name: `expert_ids`: each row names 8 different experts. In the rows of one device no expert is named more than 40 times, and one expert is named exactly 40 times in the rows of every device.
All inputs are finite; a program needn't handle non-finite values.
Results may differ from the reference program's by a relative error of at most 0.0061.
Values may be sent and summed in bfloat16 or wider, within the bound.
A program may use at most 128 MiB of HBM per device.

```python
import math
import jax
import jax.numpy as jnp
from jax import lax

D = 2048
HEADS = 16
KVH = 2
HD = 128
FFW = 768
TOP = 8
TOK_DEV = 128
GROUP = 8
STEPS = 2
EXPERTS = 32
CAP = 40
TOKENS = 32768
N_CTX = 8
N_EP = 32


def base_keys(key):
    normal_keys = jax.random.normal(jax.random.fold_in(key, 11), (TOKENS, KVH * HD), jnp.float32)
    return jnp.clip(normal_keys, -6.0, 6.0)


def draw_keys(key, part):
    values_out = base_keys(key)
    return values_out.astype(jnp.bfloat16)


def draw_queries(key, part):
    normal_q = jax.random.normal(jax.random.fold_in(key, 12), (TOKENS, HEADS * HD), jnp.float32)
    values_out = 2.0 * jnp.clip(normal_q, -6.0, 6.0)
    return values_out.astype(jnp.bfloat16)


def draw_residual(key, part):
    normal_x = jnp.clip(jax.random.normal(jax.random.fold_in(key, 21), (TOKENS, D), jnp.float32), -6.0, 6.0)
    col_scale = jnp.exp(jax.random.uniform(jax.random.fold_in(key, 22), (D,), jnp.float32, math.log(0.3), math.log(3.0)))
    row_scale = jnp.exp(jax.random.uniform(jax.random.fold_in(key, 23), (TOKENS, 1), jnp.float32, math.log(0.5), math.log(2.0)))
    values_out = 0.5 * row_scale * col_scale * normal_x
    return jnp.clip(values_out, -40.0, 40.0).astype(jnp.bfloat16)


def draw_expert_ids(key, part):
    block_count = TOKENS // TOK_DEV
    others = EXPERTS - 1
    hot_expert = jax.random.randint(jax.random.fold_in(key, 31), (), 0, EXPERTS, jnp.int32)

    def permute_rows(sub_key):
        return jax.random.permutation(sub_key, TOK_DEV).astype(jnp.int32)

    def permute_labels(sub_key):
        return jax.random.permutation(sub_key, others).astype(jnp.int32)
    row_order = jax.vmap(permute_rows)(jax.random.split(jax.random.fold_in(key, 32), block_count))
    heavy_rows = jax.vmap(permute_rows)(jax.random.split(jax.random.fold_in(key, 33), block_count)) < CAP
    labels = jax.vmap(permute_labels)(jax.random.split(jax.random.fold_in(key, 34), block_count))
    pick_steps = jnp.arange(TOP, dtype=jnp.int32)
    offsets = (row_order[:, :, None] % others + pick_steps[None, None, :]) % others

    def label_of(label_row, offset_rows):
        return label_row[offset_rows]
    picked = jax.vmap(label_of)(labels, offsets)
    names = (hot_expert + 1 + picked) % EXPERTS
    names = jnp.where(jnp.logical_and(heavy_rows[:, :, None], pick_steps[None, None, :] == TOP - 1), hot_expert, names)
    rotate = jax.random.randint(jax.random.fold_in(key, 35), (block_count, TOK_DEV, 1), 0, TOP, jnp.int32)
    names = jnp.take_along_axis(names, (pick_steps[None, None, :] + rotate) % TOP, axis=2)
    return names.reshape(TOKENS, TOP).astype(jnp.int32)


def with_spikes(drawn, stream_key, source, target, parts, factor):
    def block_of(dim):
        return (jnp.arange(drawn.shape[dim]) // (drawn.shape[dim] // parts)).reshape((-1,) + (1,) * (drawn.ndim - 1 - dim))

    near = jax.random.permutation(stream_key, parts)[block_of(target)]
    far = (block_of(target) + parts // 2) % parts
    return jnp.where((block_of(source) == near) | (block_of(source) == far), factor * drawn, drawn)


def shard_levels(key, extent, cuts, low, high):
    def one(axis_at, blocks):
        steps = jax.random.uniform(jax.random.fold_in(jax.random.fold_in(key, 6), axis_at), (blocks,), jnp.float32, low / len(cuts), high / len(cuts))
        return jnp.repeat(jnp.exp(steps), extent[axis_at] // blocks).reshape((-1,) + (1,) * (len(extent) - axis_at - 1))

    gain = one(*cuts[0])
    for cut in cuts[1:]:
        gain = gain * one(*cut)
    return gain


def centred(own_key, extent, deviation, limit, cuts=(), kind=jnp.bfloat16):
    values = deviation * jax.random.normal(own_key, extent, jnp.float32)
    if cuts:
        values = values * shard_levels(own_key, extent, cuts, -0.22, 0.18)
    return jnp.clip(values, -limit, limit).astype(kind)


def noise_with(stream_key, dims, scale, most, pieces, heavy, kind=jnp.bfloat16):
    values = scale * jax.random.normal(stream_key, dims, jnp.float32)
    if pieces:
        values = values * shard_levels(stream_key, dims, pieces, -0.22, 0.18)
    return jnp.clip(with_spikes(values, jax.random.fold_in(stream_key, 3), *heavy), -most, most).astype(kind)


def setup_inputs(seed: int = 0) -> dict:
    key_of = jax.random.split(jax.random.key(seed), 13)
    return {
        "queries": draw_queries(jax.random.fold_in(key_of[12], 71), 0),
        "keys": draw_keys(jax.random.fold_in(key_of[12], 71), 0),
        "values": centred(key_of[2], (TOKENS, KVH * HD), 1.0, 6.0, ((0, 256),)),
        "prior_out": centred(key_of[3], (TOKENS, HEADS * HD), 0.5, 6.0, ((0, 256),)),
        "prior_lse": jnp.clip(4.0 + 4.0 * jax.random.uniform(key_of[4], (TOKENS, HEADS), jnp.float32) ** shard_levels(key_of[4], (TOKENS, HEADS), ((0, 256),), -0.2, 0.2), 4.0, 8.0),
        "residual": draw_residual(jax.random.fold_in(key_of[12], 71), 0),
        "out_proj": noise_with(key_of[6], (HEADS * HD, D), (HEADS * HD) ** -0.5, 0.5, ((0, 256),), (0, 1, 256, 6.0)),
        "norm_gain": jnp.clip(1.0 + 0.1 * jax.random.normal(key_of[7], (D,), jnp.float32), 0.5, 1.5),
        "expert_in": centred(key_of[8], (EXPERTS, D, 2 * FFW), D ** -0.5, 0.125, ((0, 32),)),
        "expert_out": centred(key_of[9], (EXPERTS, FFW, D), FFW ** -0.5, 0.21875, ((0, 32),)),
        "expert_ids": draw_expert_ids(jax.random.fold_in(key_of[12], 71), 0),
        "route_weight": jnp.clip(jnp.exp(math.log(0.6) - 2.4849067 * jax.random.uniform(key_of[11], (TOKENS, TOP), jnp.float32) ** shard_levels(key_of[11], (TOKENS, TOP), ((0, 256),), -0.2, 0.2)), 0.05, 0.6),
    }


def attend_group(ctx_index, query_all, key_all, value_all, prior_all, lse_all):
    query_blk = query_all[ctx_index].reshape(N_EP, TOK_DEV, KVH, GROUP, HD).astype(jnp.float32)
    sources = [(ctx_index - stride) % N_CTX for stride in range(1, STEPS + 1)]
    key_win = jnp.concatenate([key_all[src_idx] for src_idx in sources], axis=1)
    key_win = key_win.reshape(N_EP, STEPS * TOK_DEV, KVH, HD).astype(jnp.float32)
    value_win = jnp.concatenate([value_all[src_idx] for src_idx in sources], axis=1)
    value_win = value_win.reshape(N_EP, STEPS * TOK_DEV, KVH, HD).astype(jnp.float32)
    scores = jnp.einsum('eighd,ejgd->eghij', query_blk, key_win) / math.sqrt(HD)
    query_local = jnp.arange(TOK_DEV, dtype=jnp.int32)[:, None]
    key_local = (jnp.arange(STEPS * TOK_DEV, dtype=jnp.int32) % TOK_DEV)[None, :]
    key_ctx = jnp.concatenate([jnp.zeros((TOK_DEV,), jnp.int32) + src_idx for src_idx in sources])[None, :]
    visible = (key_local < query_local) | (key_local == query_local) & (key_ctx <= ctx_index)
    scores = jnp.where(visible, scores, -jnp.inf)
    lse_prior = lse_all[ctx_index].reshape(N_EP, TOK_DEV, KVH, GROUP).transpose(0, 2, 3, 1)
    top_score = jnp.maximum(lse_prior, lax.optimization_barrier(jnp.max(scores, axis=-1)))
    weights = jnp.exp(scores - top_score[..., None])
    prior_weight = jnp.exp(lse_prior - top_score)
    totals = prior_weight + lax.optimization_barrier(jnp.sum(weights, axis=-1))
    weights_bf = lax.optimization_barrier(weights.astype(jnp.bfloat16)).astype(jnp.float32)
    gathered = jnp.einsum('eghij,ejgd->eighd', weights_bf, value_win)
    prior_part = prior_all[ctx_index].reshape(N_EP, TOK_DEV, KVH, GROUP, HD).astype(jnp.float32)
    prior_part = prior_part * prior_weight.transpose(0, 3, 1, 2)[..., None]
    result = (prior_part + gathered) / totals.transpose(0, 3, 1, 2)[..., None]
    return result.astype(jnp.bfloat16).reshape(N_EP, TOK_DEV, HEADS * HD)

def reference(queries, keys, values, prior_out, prior_lse, residual, out_proj, norm_gain, expert_in, expert_out, expert_ids, route_weight):

    def shaped(array):
        return array.reshape(N_CTX, N_EP, TOK_DEV, array.shape[-1])
    query_all = shaped(queries)
    key_all = shaped(keys)
    value_all = shaped(values)
    prior_all = shaped(prior_out)
    lse_all = shaped(prior_lse)

    def one_group(ctx_index):
        return attend_group(ctx_index, query_all, key_all, value_all, prior_all, lse_all)
    attended = lax.map(one_group, jnp.arange(N_CTX, dtype=jnp.int32)).reshape(TOKENS, HEADS * HD)
    mixed_state = (residual.astype(jnp.float32) + jnp.dot(attended, out_proj, preferred_element_type=jnp.float32)).astype(jnp.bfloat16)
    state_f = lax.optimization_barrier(mixed_state).astype(jnp.float32)
    normed = (state_f * lax.rsqrt(lax.optimization_barrier(jnp.mean(state_f * state_f, axis=-1, keepdims=True)) + 1e-06) * norm_gain).astype(jnp.bfloat16)
    flat_ids = expert_ids.reshape(-1)
    flat_weight = route_weight.reshape(-1)
    most_rows = N_CTX * N_EP * CAP

    def one_expert(summed, expert):
        chosen = flat_ids == expert
        picked = jnp.nonzero(chosen, size=most_rows, fill_value=0)[0].astype(jnp.int32)
        filled = jnp.arange(most_rows, dtype=jnp.int32) < jnp.sum(chosen.astype(jnp.int32))
        token_idx = picked // TOP
        inputs = normed[token_idx].astype(jnp.float32)
        gate_up = jnp.dot(inputs, expert_in[expert].astype(jnp.float32), preferred_element_type=jnp.float32)
        activated = (jax.nn.silu(gate_up[:, :FFW]) * gate_up[:, FFW:]).astype(jnp.bfloat16)
        replies = jnp.dot(activated.astype(jnp.float32), expert_out[expert].astype(jnp.float32), preferred_element_type=jnp.float32).astype(jnp.bfloat16)
        scaling = jnp.where(filled, flat_weight[picked], jnp.zeros((), flat_weight.dtype))
        summed = summed.at[token_idx].add(scaling[:, None] * replies.astype(jnp.float32))
        return (summed, None)
    summed, unused = lax.scan(one_expert, jnp.zeros((TOKENS, D), jnp.float32), jnp.arange(EXPERTS, dtype=jnp.int32))
    layer_out = (state_f + summed).astype(jnp.bfloat16)
    return (layer_out, attended)
```

```python
import math

import jax
import jax.numpy as jnp
from jax import lax
from jax.sharding import PartitionSpec as P

HEADS = 16
KVH = 2
HD = 128
GROUP = 8


def passed_along(shard, axis, by):
    devices = lax.axis_size(axis)
    return lax.ppermute(shard, axis, [(i, (i + by) % devices) for i in range(devices)])


def run_expert(inputs, weight_in, weight_out, hidden_units):
    flat_in = inputs.reshape(-1, inputs.shape[-1])
    gate_up = jnp.dot(flat_in, weight_in, preferred_element_type=jnp.float32)
    activated = (jax.nn.silu(gate_up[:, :hidden_units]) * gate_up[:, hidden_units:]).astype(
        jnp.bfloat16
    )
    replies = jnp.dot(activated, weight_out, preferred_element_type=jnp.float32).astype(
        jnp.bfloat16
    )
    return replies.reshape(inputs.shape[:-1] + (weight_out.shape[-1],))


def shards(
    queries,
    keys,
    values,
    prior_out,
    prior_lse,
    residual,
    out_proj,
    norm_gain,
    expert_in,
    expert_out,
    expert_ids,
    route_weight,
):
    local_rows = queries.shape[0]
    ctx_count = lax.axis_size("ctx")
    ctx_here = lax.axis_index("ctx")
    ep_count = lax.axis_size("ep")
    reach_steps = min(2, ctx_count - 1)
    kv_pair = jnp.stack([keys, values])
    arrived = []
    current = kv_pair
    for stride in range(reach_steps):
        current = passed_along(current, "ctx", 1)
        arrived.append(current)
    window = jnp.concatenate(arrived, axis=1)
    width_kv = window.shape[1]
    key_win = window[0].reshape(width_kv, KVH, HD)
    value_win = window[1].reshape(width_kv, KVH, HD)
    query_blk = queries.reshape(local_rows, KVH, GROUP, HD)
    scores = jnp.einsum(
        "ighd,jgd->ghij", query_blk, key_win, preferred_element_type=jnp.float32
    ) / math.sqrt(HD)
    positions = jnp.arange(width_kv, dtype=jnp.int32)
    key_local = positions % local_rows
    key_ctx = (ctx_here - (positions // local_rows + 1)) % ctx_count
    query_local = jnp.arange(local_rows, dtype=jnp.int32)[:, None]
    visible = (key_local[None, :] < query_local) | (key_local[None, :] == query_local) & (
        key_ctx[None, :] <= ctx_here
    )
    scores = jnp.where(visible, scores, -jnp.inf)
    lse_prior = prior_lse.reshape(local_rows, KVH, GROUP).transpose(1, 2, 0)
    top_score = jnp.maximum(lse_prior, jnp.max(scores, axis=-1))
    weights = jnp.exp(scores - top_score[..., None])
    prior_weight = jnp.exp(lse_prior - top_score)
    totals = prior_weight + jnp.sum(weights, axis=-1)
    gathered = jnp.einsum(
        "ghij,jgd->ighd",
        weights.astype(jnp.bfloat16),
        value_win,
        preferred_element_type=jnp.float32,
    )
    prior_part = (
        prior_out.reshape(local_rows, KVH, GROUP, HD).astype(jnp.float32)
        * prior_weight.transpose(2, 0, 1)[..., None]
    )
    attended = ((prior_part + gathered) / totals.transpose(2, 0, 1)[..., None]).astype(jnp.bfloat16)
    attended = attended.reshape(local_rows, HEADS * HD)
    model_width = out_proj.shape[1]
    weight_rows = lax.all_gather(
        lax.all_gather(out_proj, "ctx", axis=0, tiled=True), "ep", axis=0, tiled=True
    )
    block_rows = out_proj.shape[0]
    attended_perm = (
        attended.reshape(local_rows, ctx_count, ep_count, block_rows)
        .transpose(0, 2, 1, 3)
        .reshape(local_rows, HEADS * HD)
    )
    projected = jnp.dot(attended_perm, weight_rows, preferred_element_type=jnp.float32)
    mixed_state = (residual.astype(jnp.float32) + projected).astype(jnp.bfloat16)
    state_f = lax.optimization_barrier(mixed_state).astype(jnp.float32)
    normed = (
        state_f * lax.rsqrt(jnp.mean(state_f * state_f, axis=-1, keepdims=True) + 1e-06) * norm_gain
    ).astype(jnp.bfloat16)
    experts_all = ep_count * expert_in.shape[0]
    top_count = expert_ids.shape[1]
    capacity = max(
        local_rows // 4, top_count * ((local_rows + experts_all - 2) // (experts_all - 1))
    )
    flat_ids = expert_ids.reshape(-1)
    one_hot = (flat_ids[:, None] == jnp.arange(experts_all, dtype=jnp.int32)[None, :]).astype(
        jnp.int32
    )
    earlier = jnp.cumsum(one_hot, axis=0) - one_hot
    slot_ids = flat_ids * capacity + jnp.sum(earlier * one_hot, axis=1)
    outgoing = jnp.zeros((experts_all * capacity, model_width), jnp.bfloat16)
    outgoing = (
        outgoing.at[slot_ids]
        .set(jnp.repeat(normed, top_count, axis=0))
        .reshape(experts_all, capacity, model_width)
    )
    weight_in = expert_in[0]
    weight_out = expert_out[0]
    hidden_units = weight_out.shape[0]
    replies = run_expert(
        lax.all_to_all(outgoing, "ep", split_axis=0, concat_axis=0, tiled=True),
        weight_in,
        weight_out,
        hidden_units,
    )
    returned = lax.all_to_all(replies, "ep", split_axis=0, concat_axis=0, tiled=True)
    picked = returned.reshape(experts_all * capacity, model_width)[slot_ids].reshape(
        local_rows, top_count, model_width
    )
    combined = jnp.sum(route_weight[:, :, None] * picked.astype(jnp.float32), axis=1)
    layer_out = (state_f + combined).astype(jnp.bfloat16)
    return (layer_out, attended)


def solution(mesh):
    return jax.shard_map(
        shards,
        mesh=mesh,
        in_specs=(
            P(("ctx", "ep"), None),
            P(("ctx", "ep"), None),
            P(("ctx", "ep"), None),
            P(("ctx", "ep"), None),
            P(("ctx", "ep"), None),
            P(("ctx", "ep"), None),
            P(("ctx", "ep"), None),
            P(),
            P("ep", None, None),
            P("ep", None, None),
            P(("ctx", "ep"), None),
            P(("ctx", "ep"), None),
        ),
        out_specs=(P(("ctx", "ep"), None), P(("ctx", "ep"), None)),
        check_vma=False,
    )
```

```python
import math

import jax
import jax.numpy as jnp
from jax import lax
from jax.sharding import PartitionSpec as P

HEADS = 16
KVH = 2
HD = 128
GROUP = 8


def passed_along(shard, axis, by):
    devices = lax.axis_size(axis)
    return lax.ppermute(shard, axis, [(i, (i + by) % devices) for i in range(devices)])


def run_expert(inputs, weight_in, weight_out, hidden_units):
    flat_in = inputs.reshape(-1, inputs.shape[-1])
    gate_up = jnp.dot(flat_in, weight_in, preferred_element_type=jnp.float32)
    activated = (jax.nn.silu(gate_up[:, :hidden_units]) * gate_up[:, hidden_units:]).astype(
        jnp.bfloat16
    )
    replies = jnp.dot(activated, weight_out, preferred_element_type=jnp.float32).astype(
        jnp.bfloat16
    )
    return replies.reshape(inputs.shape[:-1] + (weight_out.shape[-1],))


def shards(
    queries,
    keys,
    values,
    prior_out,
    prior_lse,
    residual,
    out_proj,
    norm_gain,
    expert_in,
    expert_out,
    expert_ids,
    route_weight,
):
    local_rows = queries.shape[0]
    ctx_count = lax.axis_size("ctx")
    ctx_here = lax.axis_index("ctx")
    ep_count = lax.axis_size("ep")
    reach_steps = min(2, ctx_count - 1)
    kv_pair = jnp.stack([keys, values])
    arrived = []
    current = kv_pair
    for stride in range(reach_steps):
        current = passed_along(current, "ctx", 1)
        arrived.append(current)
    window = jnp.concatenate(arrived, axis=1)
    width_kv = window.shape[1]
    key_win = window[0].reshape(width_kv, KVH, HD)
    value_win = window[1].reshape(width_kv, KVH, HD)
    query_blk = queries.reshape(local_rows, KVH, GROUP, HD)
    scores = jnp.einsum(
        "ighd,jgd->ghij", query_blk, key_win, preferred_element_type=jnp.float32
    ) / math.sqrt(HD)
    positions = jnp.arange(width_kv, dtype=jnp.int32)
    key_local = positions % local_rows
    key_ctx = (ctx_here - (positions // local_rows + 1)) % ctx_count
    query_local = jnp.arange(local_rows, dtype=jnp.int32)[:, None]
    visible = (key_local[None, :] < query_local) | (key_local[None, :] == query_local) & (
        key_ctx[None, :] <= ctx_here
    )
    scores = jnp.where(visible, scores, -jnp.inf)
    lse_prior = prior_lse.reshape(local_rows, KVH, GROUP).transpose(1, 2, 0)
    top_score = jnp.maximum(lse_prior, jnp.max(scores, axis=-1))
    weights = jnp.exp(scores - top_score[..., None])
    prior_weight = jnp.exp(lse_prior - top_score)
    totals = prior_weight + jnp.sum(weights, axis=-1)
    gathered = jnp.einsum(
        "ghij,jgd->ighd",
        weights.astype(jnp.bfloat16),
        value_win,
        preferred_element_type=jnp.float32,
    )
    prior_part = (
        prior_out.reshape(local_rows, KVH, GROUP, HD).astype(jnp.float32)
        * prior_weight.transpose(2, 0, 1)[..., None]
    )
    attended = ((prior_part + gathered) / totals.transpose(2, 0, 1)[..., None]).astype(jnp.bfloat16)
    attended = attended.reshape(local_rows, HEADS * HD)
    model_width = out_proj.shape[1]
    column_half = model_width // 2
    core = ctx_here % 2
    column_rows = lax.all_gather(out_proj, "ctx", axis=0, tiled=True)
    own_half = lax.dynamic_slice_in_dim(column_rows, core * column_half, column_half, axis=1)
    own_half = lax.all_gather(own_half, "ep", axis=0, tiled=True)
    other_half = lax.ppermute(own_half, "ctx", [(i, i ^ 1) for i in range(ctx_count)])
    block_rows = out_proj.shape[0]
    attended_perm = (
        attended.reshape(local_rows, ctx_count, ep_count, block_rows)
        .transpose(0, 2, 1, 3)
        .reshape(local_rows, HEADS * HD)
    )
    own_part = jnp.dot(attended_perm, own_half, preferred_element_type=jnp.float32)
    other_part = jnp.dot(attended_perm, other_half, preferred_element_type=jnp.float32)
    projected = jnp.zeros((local_rows, model_width), jnp.float32)
    projected = lax.dynamic_update_slice_in_dim(projected, own_part, core * column_half, axis=1)
    projected = lax.dynamic_update_slice_in_dim(
        projected, other_part, (1 - core) * column_half, axis=1
    )
    mixed_state = (residual.astype(jnp.float32) + projected).astype(jnp.bfloat16)
    state_f = lax.optimization_barrier(mixed_state).astype(jnp.float32)
    normed = (
        state_f * lax.rsqrt(jnp.mean(state_f * state_f, axis=-1, keepdims=True) + 1e-06) * norm_gain
    ).astype(jnp.bfloat16)
    experts_all = ep_count * expert_in.shape[0]
    top_count = expert_ids.shape[1]
    capacity = max(
        local_rows // 4, top_count * ((local_rows + experts_all - 2) // (experts_all - 1))
    )
    flat_ids = expert_ids.reshape(-1)
    one_hot = (flat_ids[:, None] == jnp.arange(experts_all, dtype=jnp.int32)[None, :]).astype(
        jnp.int32
    )
    earlier = jnp.cumsum(one_hot, axis=0) - one_hot
    slot_ids = flat_ids * capacity + jnp.sum(earlier * one_hot, axis=1)
    outgoing = jnp.zeros((experts_all * capacity, model_width), jnp.bfloat16)
    outgoing = (
        outgoing.at[slot_ids]
        .set(jnp.repeat(normed, top_count, axis=0))
        .reshape(experts_all, capacity, model_width)
    )
    weight_in = expert_in[0]
    weight_out = expert_out[0]
    hidden_units = weight_out.shape[0]
    replies = run_expert(
        lax.all_to_all(outgoing, "ep", split_axis=0, concat_axis=0, tiled=True),
        weight_in,
        weight_out,
        hidden_units,
    )
    returned = lax.all_to_all(replies, "ep", split_axis=0, concat_axis=0, tiled=True)
    picked = returned.reshape(experts_all * capacity, model_width)[slot_ids].reshape(
        local_rows, top_count, model_width
    )
    combined = jnp.sum(route_weight[:, :, None] * picked.astype(jnp.float32), axis=1)
    layer_out = (state_f + combined).astype(jnp.bfloat16)
    return (layer_out, attended)


def solution(mesh):
    return jax.shard_map(
        shards,
        mesh=mesh,
        in_specs=(
            P(("ctx", "ep"), None),
            P(("ctx", "ep"), None),
            P(("ctx", "ep"), None),
            P(("ctx", "ep"), None),
            P(("ctx", "ep"), None),
            P(("ctx", "ep"), None),
            P(("ctx", "ep"), None),
            P(),
            P("ep", None, None),
            P("ep", None, None),
            P(("ctx", "ep"), None),
            P(("ctx", "ep"), None),
        ),
        out_specs=(P(("ctx", "ep"), None), P(("ctx", "ep"), None)),
        check_vma=False,
    )
```

```python
import functools
import math

import jax
import jax.numpy as jnp
from jax import lax
from jax.experimental import pallas as pl
from jax.experimental.pallas import tpu as pltpu
from jax.sharding import PartitionSpec as P

MESH = pl.DeviceIdType.MESH

HEADS = 16
KVH = 2
HD = 128
GROUP = 8


def passed_along(shard, axis, by):
    devices = lax.axis_size(axis)
    return lax.ppermute(shard, axis, [(i, (i + by) % devices) for i in range(devices)])


def exchange_kernel(per_peer, src_ref, dst_ref, send_sem, recv_sem, local_sem):
    n_ep = lax.axis_size("ep")
    n_ctx = lax.axis_size("ctx")
    me = lax.axis_index("ep")
    ctx_me = lax.axis_index("ctx")
    ctx_far = (ctx_me + n_ctx // 2) % n_ctx

    def peer(j):
        p = (me + j) % n_ep
        same = 1 - (p + me) % 2
        return p, same * ctx_me + (1 - same) * ctx_far

    def chunk(p):
        return src_ref.at[p] if per_peer else src_ref.at[0]

    barrier = pltpu.get_barrier_semaphore()

    def greet(j, carry):
        p, c = peer(j)
        pl.semaphore_signal(barrier, inc=1, device_id=(c, p), device_id_type=MESH)
        return carry

    lax.fori_loop(1, n_ep, greet, 0)
    pl.semaphore_wait(barrier, n_ep - 1)

    local = pltpu.make_async_copy(chunk(me), dst_ref.at[me], local_sem)
    local.start()

    def send(j, carry):
        p, c = peer(j)
        pltpu.make_async_remote_copy(
            src_ref=chunk(p),
            dst_ref=dst_ref.at[me],
            send_sem=send_sem.at[p],
            recv_sem=recv_sem.at[me],
            device_id=(c, p),
            device_id_type=MESH,
        ).start()
        return carry

    lax.fori_loop(1, n_ep, send, 0)

    def finish(j, carry):
        p, c = peer(j)
        pltpu.make_async_remote_copy(
            src_ref=chunk(p),
            dst_ref=dst_ref.at[me],
            send_sem=send_sem.at[p],
            recv_sem=recv_sem.at[me],
            device_id=(c, p),
            device_id_type=MESH,
        ).wait_send()
        pltpu.make_async_remote_copy(
            src_ref=chunk(p),
            dst_ref=dst_ref.at[p],
            send_sem=send_sem.at[p],
            recv_sem=recv_sem.at[p],
            device_id=(c, p),
            device_id_type=MESH,
        ).wait_recv()
        return carry

    lax.fori_loop(1, n_ep, finish, 0)
    local.wait()


def exchange(src, per_peer, collective_id):
    n_ep = lax.axis_size("ep")
    block = src.shape[1:]
    moved = n_ep * math.prod(block) * src.dtype.itemsize
    return pl.pallas_call(
        functools.partial(exchange_kernel, per_peer),
        out_shape=jax.ShapeDtypeStruct((n_ep,) + block, src.dtype),
        in_specs=[pl.BlockSpec(memory_space=pl.ANY)],
        out_specs=pl.BlockSpec(memory_space=pl.ANY),
        scratch_shapes=[
            pltpu.SemaphoreType.DMA((n_ep,)),
            pltpu.SemaphoreType.DMA((n_ep,)),
            pltpu.SemaphoreType.DMA,
        ],
        compiler_params=pltpu.CompilerParams(
            collective_id=collective_id, has_side_effects=True
        ),
        cost_estimate=pl.CostEstimate(flops=0, transcendentals=0, bytes_accessed=2 * moved),
    )(src)


def run_expert(inputs, weight_in, weight_out, hidden_units):
    flat_in = inputs.reshape(-1, inputs.shape[-1])
    gate_up = jnp.dot(flat_in, weight_in, preferred_element_type=jnp.float32)
    activated = (jax.nn.silu(gate_up[:, :hidden_units]) * gate_up[:, hidden_units:]).astype(
        jnp.bfloat16
    )
    replies = jnp.dot(activated, weight_out, preferred_element_type=jnp.float32).astype(
        jnp.bfloat16
    )
    return replies.reshape(inputs.shape[:-1] + (weight_out.shape[-1],))


def shards(
    queries,
    keys,
    values,
    prior_out,
    prior_lse,
    residual,
    out_proj,
    norm_gain,
    expert_in,
    expert_out,
    expert_ids,
    route_weight,
):
    local_rows = queries.shape[0]
    ctx_count = lax.axis_size("ctx")
    ctx_here = lax.axis_index("ctx")
    ep_count = lax.axis_size("ep")
    reach_steps = min(2, ctx_count - 1)
    kv_pair = jnp.stack([keys, values])
    arrived = []
    current = kv_pair
    for stride in range(reach_steps):
        current = passed_along(current, "ctx", 1)
        arrived.append(current)
    window = jnp.concatenate(arrived, axis=1)
    width_kv = window.shape[1]
    key_win = window[0].reshape(width_kv, KVH, HD)
    value_win = window[1].reshape(width_kv, KVH, HD)
    query_blk = queries.reshape(local_rows, KVH, GROUP, HD)
    scores = jnp.einsum(
        "ighd,jgd->ghij", query_blk, key_win, preferred_element_type=jnp.float32
    ) / math.sqrt(HD)
    positions = jnp.arange(width_kv, dtype=jnp.int32)
    key_local = positions % local_rows
    key_ctx = (ctx_here - (positions // local_rows + 1)) % ctx_count
    query_local = jnp.arange(local_rows, dtype=jnp.int32)[:, None]
    visible = (key_local[None, :] < query_local) | (key_local[None, :] == query_local) & (
        key_ctx[None, :] <= ctx_here
    )
    scores = jnp.where(visible, scores, -jnp.inf)
    lse_prior = prior_lse.reshape(local_rows, KVH, GROUP).transpose(1, 2, 0)
    top_score = jnp.maximum(lse_prior, jnp.max(scores, axis=-1))
    weights = jnp.exp(scores - top_score[..., None])
    prior_weight = jnp.exp(lse_prior - top_score)
    totals = prior_weight + jnp.sum(weights, axis=-1)
    gathered = jnp.einsum(
        "ghij,jgd->ighd",
        weights.astype(jnp.bfloat16),
        value_win,
        preferred_element_type=jnp.float32,
    )
    prior_part = (
        prior_out.reshape(local_rows, KVH, GROUP, HD).astype(jnp.float32)
        * prior_weight.transpose(2, 0, 1)[..., None]
    )
    attended = ((prior_part + gathered) / totals.transpose(2, 0, 1)[..., None]).astype(jnp.bfloat16)
    attended = attended.reshape(local_rows, HEADS * HD)
    model_width = out_proj.shape[1]
    column_half = model_width // 2
    core = ctx_here % 2
    column_rows = lax.all_gather(out_proj, "ctx", axis=0, tiled=True)
    own_half = lax.dynamic_slice_in_dim(column_rows, core * column_half, column_half, axis=1)
    own_half = exchange(own_half[None], False, 0).reshape(-1, column_half)
    other_half = lax.ppermute(own_half, "ctx", [(i, i ^ 1) for i in range(ctx_count)])
    block_rows = out_proj.shape[0]
    attended_perm = (
        attended.reshape(local_rows, ctx_count, ep_count, block_rows)
        .transpose(0, 2, 1, 3)
        .reshape(local_rows, HEADS * HD)
    )
    own_part = jnp.dot(attended_perm, own_half, preferred_element_type=jnp.float32)
    other_part = jnp.dot(attended_perm, other_half, preferred_element_type=jnp.float32)
    projected = jnp.zeros((local_rows, model_width), jnp.float32)
    projected = lax.dynamic_update_slice_in_dim(projected, own_part, core * column_half, axis=1)
    projected = lax.dynamic_update_slice_in_dim(
        projected, other_part, (1 - core) * column_half, axis=1
    )
    mixed_state = (residual.astype(jnp.float32) + projected).astype(jnp.bfloat16)
    state_f = lax.optimization_barrier(mixed_state).astype(jnp.float32)
    normed = (
        state_f * lax.rsqrt(jnp.mean(state_f * state_f, axis=-1, keepdims=True) + 1e-06) * norm_gain
    ).astype(jnp.bfloat16)
    experts_all = ep_count * expert_in.shape[0]
    top_count = expert_ids.shape[1]
    capacity = max(
        local_rows // 4, top_count * ((local_rows + experts_all - 2) // (experts_all - 1))
    )
    flat_ids = expert_ids.reshape(-1)
    one_hot = (flat_ids[:, None] == jnp.arange(experts_all, dtype=jnp.int32)[None, :]).astype(
        jnp.int32
    )
    earlier = jnp.cumsum(one_hot, axis=0) - one_hot
    slot_ids = flat_ids * capacity + jnp.sum(earlier * one_hot, axis=1)
    outgoing = jnp.zeros((experts_all * capacity, model_width), jnp.bfloat16)
    outgoing = (
        outgoing.at[slot_ids]
        .set(jnp.repeat(normed, top_count, axis=0))
        .reshape(experts_all, capacity, model_width)
    )
    weight_in = expert_in[0]
    weight_out = expert_out[0]
    hidden_units = weight_out.shape[0]
    replies = run_expert(
        lax.all_to_all(outgoing, "ep", split_axis=0, concat_axis=0, tiled=True),
        weight_in,
        weight_out,
        hidden_units,
    )
    returned = lax.all_to_all(replies, "ep", split_axis=0, concat_axis=0, tiled=True)
    picked = returned.reshape(experts_all * capacity, model_width)[slot_ids].reshape(
        local_rows, top_count, model_width
    )
    combined = jnp.sum(route_weight[:, :, None] * picked.astype(jnp.float32), axis=1)
    layer_out = (state_f + combined).astype(jnp.bfloat16)
    return (layer_out, attended)


def solution(mesh):
    return jax.shard_map(
        shards,
        mesh=mesh,
        in_specs=(
            P(("ctx", "ep"), None),
            P(("ctx", "ep"), None),
            P(("ctx", "ep"), None),
            P(("ctx", "ep"), None),
            P(("ctx", "ep"), None),
            P(("ctx", "ep"), None),
            P(("ctx", "ep"), None),
            P(),
            P("ep", None, None),
            P("ep", None, None),
            P(("ctx", "ep"), None),
            P(("ctx", "ep"), None),
        ),
        out_specs=(P(("ctx", "ep"), None), P(("ctx", "ep"), None)),
        check_vma=False,
    )
```

```python
import functools
import math

import jax
import jax.numpy as jnp
from jax import lax
from jax.experimental import pallas as pl
from jax.experimental.pallas import tpu as pltpu
from jax.sharding import PartitionSpec as P

MESH = pl.DeviceIdType.MESH

HEADS = 16
KVH = 2
HD = 128
GROUP = 8


def passed_along(shard, axis, by):
    devices = lax.axis_size(axis)
    return lax.ppermute(shard, axis, [(i, (i + by) % devices) for i in range(devices)])


def exchange_kernel(per_peer, src_ref, dst_ref, send_sem, recv_sem, local_sem):
    n_ep = lax.axis_size("ep")
    n_ctx = lax.axis_size("ctx")
    me = lax.axis_index("ep")
    ctx_me = lax.axis_index("ctx")
    ctx_far = (ctx_me + n_ctx // 2) % n_ctx

    def peer(j):
        p = (me + j) % n_ep
        same = 1 - (p + me) % 2
        return p, same * ctx_me + (1 - same) * ctx_far

    def chunk(p):
        return src_ref.at[p] if per_peer else src_ref.at[0]

    barrier = pltpu.get_barrier_semaphore()

    def greet(j, carry):
        p, c = peer(j)
        pl.semaphore_signal(barrier, inc=1, device_id=(c, p), device_id_type=MESH)
        return carry

    lax.fori_loop(1, n_ep, greet, 0)
    pl.semaphore_wait(barrier, n_ep - 1)

    local = pltpu.make_async_copy(chunk(me), dst_ref.at[me], local_sem)
    local.start()

    def send(j, carry):
        p, c = peer(j)
        pltpu.make_async_remote_copy(
            src_ref=chunk(p),
            dst_ref=dst_ref.at[me],
            send_sem=send_sem.at[p],
            recv_sem=recv_sem.at[me],
            device_id=(c, p),
            device_id_type=MESH,
        ).start()
        return carry

    lax.fori_loop(1, n_ep, send, 0)

    def finish(j, carry):
        p, c = peer(j)
        pltpu.make_async_remote_copy(
            src_ref=chunk(p),
            dst_ref=dst_ref.at[me],
            send_sem=send_sem.at[p],
            recv_sem=recv_sem.at[me],
            device_id=(c, p),
            device_id_type=MESH,
        ).wait_send()
        pltpu.make_async_remote_copy(
            src_ref=chunk(p),
            dst_ref=dst_ref.at[p],
            send_sem=send_sem.at[p],
            recv_sem=recv_sem.at[p],
            device_id=(c, p),
            device_id_type=MESH,
        ).wait_recv()
        return carry

    lax.fori_loop(1, n_ep, finish, 0)
    local.wait()


def exchange(src, per_peer, collective_id):
    n_ep = lax.axis_size("ep")
    block = src.shape[1:]
    moved = n_ep * math.prod(block) * src.dtype.itemsize
    return pl.pallas_call(
        functools.partial(exchange_kernel, per_peer),
        out_shape=jax.ShapeDtypeStruct((n_ep,) + block, src.dtype),
        in_specs=[pl.BlockSpec(memory_space=pl.ANY)],
        out_specs=pl.BlockSpec(memory_space=pl.ANY),
        scratch_shapes=[
            pltpu.SemaphoreType.DMA((n_ep,)),
            pltpu.SemaphoreType.DMA((n_ep,)),
            pltpu.SemaphoreType.DMA,
        ],
        compiler_params=pltpu.CompilerParams(
            collective_id=collective_id, has_side_effects=True
        ),
        cost_estimate=pl.CostEstimate(flops=0, transcendentals=0, bytes_accessed=2 * moved),
    )(src)


def run_expert(inputs, weight_in, weight_out, hidden_units):
    flat_in = inputs.reshape(-1, inputs.shape[-1])
    gate_up = jnp.dot(flat_in, weight_in, preferred_element_type=jnp.float32)
    activated = (jax.nn.silu(gate_up[:, :hidden_units]) * gate_up[:, hidden_units:]).astype(
        jnp.bfloat16
    )
    replies = jnp.dot(activated, weight_out, preferred_element_type=jnp.float32).astype(
        jnp.bfloat16
    )
    return replies.reshape(inputs.shape[:-1] + (weight_out.shape[-1],))


def shards(
    queries,
    keys,
    values,
    prior_out,
    prior_lse,
    residual,
    out_proj,
    norm_gain,
    expert_in,
    expert_out,
    expert_ids,
    route_weight,
):
    local_rows = queries.shape[0]
    ctx_count = lax.axis_size("ctx")
    ctx_here = lax.axis_index("ctx")
    ep_count = lax.axis_size("ep")
    reach_steps = min(2, ctx_count - 1)
    kv_pair = jnp.stack([keys, values])
    arrived = []
    current = kv_pair
    for stride in range(reach_steps):
        current = passed_along(current, "ctx", 1)
        arrived.append(current)
    window = jnp.concatenate(arrived, axis=1)
    width_kv = window.shape[1]
    key_win = window[0].reshape(width_kv, KVH, HD)
    value_win = window[1].reshape(width_kv, KVH, HD)
    query_blk = queries.reshape(local_rows, KVH, GROUP, HD)
    scores = jnp.einsum(
        "ighd,jgd->ghij", query_blk, key_win, preferred_element_type=jnp.float32
    ) / math.sqrt(HD)
    positions = jnp.arange(width_kv, dtype=jnp.int32)
    key_local = positions % local_rows
    key_ctx = (ctx_here - (positions // local_rows + 1)) % ctx_count
    query_local = jnp.arange(local_rows, dtype=jnp.int32)[:, None]
    visible = (key_local[None, :] < query_local) | (key_local[None, :] == query_local) & (
        key_ctx[None, :] <= ctx_here
    )
    scores = jnp.where(visible, scores, -jnp.inf)
    lse_prior = prior_lse.reshape(local_rows, KVH, GROUP).transpose(1, 2, 0)
    top_score = jnp.maximum(lse_prior, jnp.max(scores, axis=-1))
    weights = jnp.exp(scores - top_score[..., None])
    prior_weight = jnp.exp(lse_prior - top_score)
    totals = prior_weight + jnp.sum(weights, axis=-1)
    gathered = jnp.einsum(
        "ghij,jgd->ighd",
        weights.astype(jnp.bfloat16),
        value_win,
        preferred_element_type=jnp.float32,
    )
    prior_part = (
        prior_out.reshape(local_rows, KVH, GROUP, HD).astype(jnp.float32)
        * prior_weight.transpose(2, 0, 1)[..., None]
    )
    attended = ((prior_part + gathered) / totals.transpose(2, 0, 1)[..., None]).astype(jnp.bfloat16)
    attended = attended.reshape(local_rows, HEADS * HD)
    model_width = out_proj.shape[1]
    column_half = model_width // 2
    core = ctx_here % 2
    column_rows = lax.all_gather(out_proj, "ctx", axis=0, tiled=True)
    own_half = lax.dynamic_slice_in_dim(column_rows, core * column_half, column_half, axis=1)
    own_half = exchange(own_half[None], False, 0).reshape(-1, column_half)
    other_half = lax.ppermute(own_half, "ctx", [(i, i ^ 1) for i in range(ctx_count)])
    block_rows = out_proj.shape[0]
    attended_perm = (
        attended.reshape(local_rows, ctx_count, ep_count, block_rows)
        .transpose(0, 2, 1, 3)
        .reshape(local_rows, HEADS * HD)
    )
    own_part = jnp.dot(attended_perm, own_half, preferred_element_type=jnp.float32)
    other_part = jnp.dot(attended_perm, other_half, preferred_element_type=jnp.float32)
    projected = jnp.zeros((local_rows, model_width), jnp.float32)
    projected = lax.dynamic_update_slice_in_dim(projected, own_part, core * column_half, axis=1)
    projected = lax.dynamic_update_slice_in_dim(
        projected, other_part, (1 - core) * column_half, axis=1
    )
    mixed_state = (residual.astype(jnp.float32) + projected).astype(jnp.bfloat16)
    state_f = lax.optimization_barrier(mixed_state).astype(jnp.float32)
    normed = (
        state_f * lax.rsqrt(jnp.mean(state_f * state_f, axis=-1, keepdims=True) + 1e-06) * norm_gain
    ).astype(jnp.bfloat16)
    experts_all = ep_count * expert_in.shape[0]
    top_count = expert_ids.shape[1]
    capacity = max(
        local_rows // 4, top_count * ((local_rows + experts_all - 2) // (experts_all - 1))
    )
    flat_ids = expert_ids.reshape(-1)
    one_hot = (flat_ids[:, None] == jnp.arange(experts_all, dtype=jnp.int32)[None, :]).astype(
        jnp.int32
    )
    earlier = jnp.cumsum(one_hot, axis=0) - one_hot
    slot_ids = flat_ids * capacity + jnp.sum(earlier * one_hot, axis=1)
    outgoing = jnp.zeros((experts_all * capacity, model_width), jnp.bfloat16)
    outgoing = (
        outgoing.at[slot_ids]
        .set(jnp.repeat(normed, top_count, axis=0))
        .reshape(experts_all, capacity, model_width)
    )
    weight_in = expert_in[0]
    weight_out = expert_out[0]
    hidden_units = weight_out.shape[0]
    replies = run_expert(
        exchange(outgoing, True, 1),
        weight_in,
        weight_out,
        hidden_units,
    )
    returned = exchange(replies, True, 2)
    picked = returned.reshape(experts_all * capacity, model_width)[slot_ids].reshape(
        local_rows, top_count, model_width
    )
    combined = jnp.sum(route_weight[:, :, None] * picked.astype(jnp.float32), axis=1)
    layer_out = (state_f + combined).astype(jnp.bfloat16)
    return (layer_out, attended)


def solution(mesh):
    return jax.shard_map(
        shards,
        mesh=mesh,
        in_specs=(
            P(("ctx", "ep"), None),
            P(("ctx", "ep"), None),
            P(("ctx", "ep"), None),
            P(("ctx", "ep"), None),
            P(("ctx", "ep"), None),
            P(("ctx", "ep"), None),
            P(("ctx", "ep"), None),
            P(),
            P("ep", None, None),
            P("ep", None, None),
            P(("ctx", "ep"), None),
            P(("ctx", "ep"), None),
        ),
        out_specs=(P(("ctx", "ep"), None), P(("ctx", "ep"), None)),
        check_vma=False,
    )
```

```python
import functools
import math

import jax
import jax.numpy as jnp
from jax import lax
from jax.experimental import pallas as pl
from jax.experimental.pallas import tpu as pltpu
from jax.sharding import PartitionSpec as P

MESH = pl.DeviceIdType.MESH

HEADS = 16
KVH = 2
HD = 128
GROUP = 8


def passed_along(shard, axis, by):
    devices = lax.axis_size(axis)
    return lax.ppermute(shard, axis, [(i, (i + by) % devices) for i in range(devices)])


def exchange_kernel(per_peer, src_ref, out_ref, dst_ref, send_sem, recv_sem, local_sem):
    n_ep = lax.axis_size("ep")
    n_ctx = lax.axis_size("ctx")
    me = lax.axis_index("ep")
    ctx_me = lax.axis_index("ctx")
    ctx_far = (ctx_me + n_ctx // 2) % n_ctx

    def peer(j):
        p = (me + j) % n_ep
        same = 1 - (p + me) % 2
        return p, same * ctx_me + (1 - same) * ctx_far

    def chunk(p):
        return src_ref.at[p] if per_peer else src_ref.at[0]

    barrier = pltpu.get_barrier_semaphore()

    def greet(j, carry):
        p, c = peer(j)
        pl.semaphore_signal(barrier, inc=1, device_id=(c, p), device_id_type=MESH)
        return carry

    lax.fori_loop(1, n_ep, greet, 0)
    pl.semaphore_wait(barrier, n_ep - 1)

    local = pltpu.make_async_copy(chunk(me), dst_ref.at[me], local_sem)
    local.start()

    def send(j, carry):
        p, c = peer(j)
        pltpu.make_async_remote_copy(
            src_ref=chunk(p),
            dst_ref=dst_ref.at[me],
            send_sem=send_sem.at[p],
            recv_sem=recv_sem.at[me],
            device_id=(c, p),
            device_id_type=MESH,
        ).start()
        return carry

    lax.fori_loop(1, n_ep, send, 0)

    def finish(j, carry):
        p, c = peer(j)
        pltpu.make_async_remote_copy(
            src_ref=chunk(p),
            dst_ref=dst_ref.at[me],
            send_sem=send_sem.at[p],
            recv_sem=recv_sem.at[me],
            device_id=(c, p),
            device_id_type=MESH,
        ).wait_send()
        pltpu.make_async_remote_copy(
            src_ref=chunk(p),
            dst_ref=dst_ref.at[p],
            send_sem=send_sem.at[p],
            recv_sem=recv_sem.at[p],
            device_id=(c, p),
            device_id_type=MESH,
        ).wait_recv()
        return carry

    lax.fori_loop(1, n_ep, finish, 0)
    local.wait()
    flush = pltpu.make_async_copy(dst_ref, out_ref, local_sem)
    flush.start()
    flush.wait()


def exchange(src, per_peer, collective_id):
    n_ep = lax.axis_size("ep")
    block = src.shape[1:]
    moved = n_ep * math.prod(block) * src.dtype.itemsize
    return pl.pallas_call(
        functools.partial(exchange_kernel, per_peer),
        out_shape=jax.ShapeDtypeStruct((n_ep,) + block, src.dtype),
        in_specs=[pl.BlockSpec(memory_space=pltpu.VMEM)],
        out_specs=pl.BlockSpec(memory_space=pl.ANY),
        scratch_shapes=[
            pltpu.VMEM((n_ep,) + block, src.dtype),
            pltpu.SemaphoreType.DMA((n_ep,)),
            pltpu.SemaphoreType.DMA((n_ep,)),
            pltpu.SemaphoreType.DMA,
        ],
        compiler_params=pltpu.CompilerParams(
            collective_id=collective_id, has_side_effects=True
        ),
        cost_estimate=pl.CostEstimate(flops=0, transcendentals=0, bytes_accessed=2 * moved),
    )(src)


def run_expert(inputs, weight_in, weight_out, hidden_units):
    flat_in = inputs.reshape(-1, inputs.shape[-1])
    gate_up = jnp.dot(flat_in, weight_in, preferred_element_type=jnp.float32)
    activated = (jax.nn.silu(gate_up[:, :hidden_units]) * gate_up[:, hidden_units:]).astype(
        jnp.bfloat16
    )
    replies = jnp.dot(activated, weight_out, preferred_element_type=jnp.float32).astype(
        jnp.bfloat16
    )
    return replies.reshape(inputs.shape[:-1] + (weight_out.shape[-1],))


def shards(
    queries,
    keys,
    values,
    prior_out,
    prior_lse,
    residual,
    out_proj,
    norm_gain,
    expert_in,
    expert_out,
    expert_ids,
    route_weight,
):
    local_rows = queries.shape[0]
    ctx_count = lax.axis_size("ctx")
    ctx_here = lax.axis_index("ctx")
    ep_count = lax.axis_size("ep")
    reach_steps = min(2, ctx_count - 1)
    kv_pair = jnp.stack([keys, values])
    arrived = []
    current = kv_pair
    for stride in range(reach_steps):
        current = passed_along(current, "ctx", 1)
        arrived.append(current)
    window = jnp.concatenate(arrived, axis=1)
    width_kv = window.shape[1]
    key_win = window[0].reshape(width_kv, KVH, HD)
    value_win = window[1].reshape(width_kv, KVH, HD)
    query_blk = queries.reshape(local_rows, KVH, GROUP, HD)
    scores = jnp.einsum(
        "ighd,jgd->ghij", query_blk, key_win, preferred_element_type=jnp.float32
    ) / math.sqrt(HD)
    positions = jnp.arange(width_kv, dtype=jnp.int32)
    key_local = positions % local_rows
    key_ctx = (ctx_here - (positions // local_rows + 1)) % ctx_count
    query_local = jnp.arange(local_rows, dtype=jnp.int32)[:, None]
    visible = (key_local[None, :] < query_local) | (key_local[None, :] == query_local) & (
        key_ctx[None, :] <= ctx_here
    )
    scores = jnp.where(visible, scores, -jnp.inf)
    lse_prior = prior_lse.reshape(local_rows, KVH, GROUP).transpose(1, 2, 0)
    top_score = jnp.maximum(lse_prior, jnp.max(scores, axis=-1))
    weights = jnp.exp(scores - top_score[..., None])
    prior_weight = jnp.exp(lse_prior - top_score)
    totals = prior_weight + jnp.sum(weights, axis=-1)
    gathered = jnp.einsum(
        "ghij,jgd->ighd",
        weights.astype(jnp.bfloat16),
        value_win,
        preferred_element_type=jnp.float32,
    )
    prior_part = (
        prior_out.reshape(local_rows, KVH, GROUP, HD).astype(jnp.float32)
        * prior_weight.transpose(2, 0, 1)[..., None]
    )
    attended = ((prior_part + gathered) / totals.transpose(2, 0, 1)[..., None]).astype(jnp.bfloat16)
    attended = attended.reshape(local_rows, HEADS * HD)
    model_width = out_proj.shape[1]
    column_half = model_width // 2
    core = ctx_here % 2
    column_rows = lax.all_gather(out_proj, "ctx", axis=0, tiled=True)
    own_half = lax.dynamic_slice_in_dim(column_rows, core * column_half, column_half, axis=1)
    own_half = exchange(own_half[None], False, 0).reshape(-1, column_half)
    other_half = lax.ppermute(own_half, "ctx", [(i, i ^ 1) for i in range(ctx_count)])
    block_rows = out_proj.shape[0]
    attended_perm = (
        attended.reshape(local_rows, ctx_count, ep_count, block_rows)
        .transpose(0, 2, 1, 3)
        .reshape(local_rows, HEADS * HD)
    )
    own_part = jnp.dot(attended_perm, own_half, preferred_element_type=jnp.float32)
    other_part = jnp.dot(attended_perm, other_half, preferred_element_type=jnp.float32)
    projected = jnp.zeros((local_rows, model_width), jnp.float32)
    projected = lax.dynamic_update_slice_in_dim(projected, own_part, core * column_half, axis=1)
    projected = lax.dynamic_update_slice_in_dim(
        projected, other_part, (1 - core) * column_half, axis=1
    )
    mixed_state = (residual.astype(jnp.float32) + projected).astype(jnp.bfloat16)
    state_f = lax.optimization_barrier(mixed_state).astype(jnp.float32)
    normed = (
        state_f * lax.rsqrt(jnp.mean(state_f * state_f, axis=-1, keepdims=True) + 1e-06) * norm_gain
    ).astype(jnp.bfloat16)
    experts_all = ep_count * expert_in.shape[0]
    top_count = expert_ids.shape[1]
    capacity = max(
        local_rows // 4, top_count * ((local_rows + experts_all - 2) // (experts_all - 1))
    )
    flat_ids = expert_ids.reshape(-1)
    one_hot = (flat_ids[:, None] == jnp.arange(experts_all, dtype=jnp.int32)[None, :]).astype(
        jnp.int32
    )
    earlier = jnp.cumsum(one_hot, axis=0) - one_hot
    slot_ids = flat_ids * capacity + jnp.sum(earlier * one_hot, axis=1)
    outgoing = jnp.zeros((experts_all * capacity, model_width), jnp.bfloat16)
    outgoing = (
        outgoing.at[slot_ids]
        .set(jnp.repeat(normed, top_count, axis=0))
        .reshape(experts_all, capacity, model_width)
    )
    weight_in = expert_in[0]
    weight_out = expert_out[0]
    hidden_units = weight_out.shape[0]
    replies = run_expert(
        exchange(outgoing, True, 1),
        weight_in,
        weight_out,
        hidden_units,
    )
    returned = exchange(replies, True, 2)
    picked = returned.reshape(experts_all * capacity, model_width)[slot_ids].reshape(
        local_rows, top_count, model_width
    )
    combined = jnp.sum(route_weight[:, :, None] * picked.astype(jnp.float32), axis=1)
    layer_out = (state_f + combined).astype(jnp.bfloat16)
    return (layer_out, attended)


def solution(mesh):
    return jax.shard_map(
        shards,
        mesh=mesh,
        in_specs=(
            P(("ctx", "ep"), None),
            P(("ctx", "ep"), None),
            P(("ctx", "ep"), None),
            P(("ctx", "ep"), None),
            P(("ctx", "ep"), None),
            P(("ctx", "ep"), None),
            P(("ctx", "ep"), None),
            P(),
            P("ep", None, None),
            P("ep", None, None),
            P(("ctx", "ep"), None),
            P(("ctx", "ep"), None),
        ),
        out_specs=(P(("ctx", "ep"), None), P(("ctx", "ep"), None)),
        check_vma=False,
    )
```

```python
import functools
import math

import jax
import jax.numpy as jnp
from jax import lax
from jax.experimental import pallas as pl
from jax.experimental.pallas import tpu as pltpu
from jax.sharding import PartitionSpec as P

MESH = pl.DeviceIdType.MESH

HEADS = 16
KVH = 2
HD = 128
GROUP = 8


def passed_along(shard, axis, by):
    devices = lax.axis_size(axis)
    return lax.ppermute(shard, axis, [(i, (i + by) % devices) for i in range(devices)])


def exchange_kernel(per_peer, src_ref, dst_ref, send_sem, recv_sem, local_sem):
    n_ep = lax.axis_size("ep")
    n_ctx = lax.axis_size("ctx")
    me = lax.axis_index("ep")
    ctx_me = lax.axis_index("ctx")
    ctx_far = (ctx_me + n_ctx // 2) % n_ctx

    core = ctx_me % 2

    def peer(j):
        p = (me + j + core * (n_ep - 2 * j)) % n_ep
        same = 1 - (p + me) % 2
        return p, same * ctx_me + (1 - same) * ctx_far

    def chunk(p):
        return src_ref.at[p] if per_peer else src_ref.at[0]

    barrier = pltpu.get_barrier_semaphore()

    def greet(j, carry):
        p, c = peer(j)
        pl.semaphore_signal(barrier, inc=1, device_id=(c, p), device_id_type=MESH)
        return carry

    lax.fori_loop(1, n_ep, greet, 0)
    pl.semaphore_wait(barrier, n_ep - 1)

    local = pltpu.make_async_copy(chunk(me), dst_ref.at[me], local_sem)
    local.start()

    def send(j, carry):
        p, c = peer(j)
        pltpu.make_async_remote_copy(
            src_ref=chunk(p),
            dst_ref=dst_ref.at[me],
            send_sem=send_sem.at[p],
            recv_sem=recv_sem.at[me],
            device_id=(c, p),
            device_id_type=MESH,
        ).start()
        return carry

    lax.fori_loop(1, n_ep, send, 0)

    def finish(j, carry):
        p, c = peer(j)
        pltpu.make_async_remote_copy(
            src_ref=chunk(p),
            dst_ref=dst_ref.at[me],
            send_sem=send_sem.at[p],
            recv_sem=recv_sem.at[me],
            device_id=(c, p),
            device_id_type=MESH,
        ).wait_send()
        pltpu.make_async_remote_copy(
            src_ref=chunk(p),
            dst_ref=dst_ref.at[p],
            send_sem=send_sem.at[p],
            recv_sem=recv_sem.at[p],
            device_id=(c, p),
            device_id_type=MESH,
        ).wait_recv()
        return carry

    lax.fori_loop(1, n_ep, finish, 0)
    local.wait()


def exchange(src, per_peer, collective_id):
    n_ep = lax.axis_size("ep")
    block = src.shape[1:]
    moved = n_ep * math.prod(block) * src.dtype.itemsize
    return pl.pallas_call(
        functools.partial(exchange_kernel, per_peer),
        out_shape=jax.ShapeDtypeStruct((n_ep,) + block, src.dtype),
        in_specs=[pl.BlockSpec(memory_space=pl.ANY)],
        out_specs=pl.BlockSpec(memory_space=pl.ANY),
        scratch_shapes=[
            pltpu.SemaphoreType.DMA((n_ep,)),
            pltpu.SemaphoreType.DMA((n_ep,)),
            pltpu.SemaphoreType.DMA,
        ],
        compiler_params=pltpu.CompilerParams(
            collective_id=collective_id, has_side_effects=True
        ),
        cost_estimate=pl.CostEstimate(flops=0, transcendentals=0, bytes_accessed=2 * moved),
    )(src)


def run_expert(inputs, weight_in, weight_out, hidden_units):
    flat_in = inputs.reshape(-1, inputs.shape[-1])
    gate_up = jnp.dot(flat_in, weight_in, preferred_element_type=jnp.float32)
    activated = (jax.nn.silu(gate_up[:, :hidden_units]) * gate_up[:, hidden_units:]).astype(
        jnp.bfloat16
    )
    replies = jnp.dot(activated, weight_out, preferred_element_type=jnp.float32).astype(
        jnp.bfloat16
    )
    return replies.reshape(inputs.shape[:-1] + (weight_out.shape[-1],))


def shards(
    queries,
    keys,
    values,
    prior_out,
    prior_lse,
    residual,
    out_proj,
    norm_gain,
    expert_in,
    expert_out,
    expert_ids,
    route_weight,
):
    local_rows = queries.shape[0]
    ctx_count = lax.axis_size("ctx")
    ctx_here = lax.axis_index("ctx")
    ep_count = lax.axis_size("ep")
    reach_steps = min(2, ctx_count - 1)
    kv_pair = jnp.stack([keys, values])
    arrived = []
    current = kv_pair
    for stride in range(reach_steps):
        current = passed_along(current, "ctx", 1)
        arrived.append(current)
    window = jnp.concatenate(arrived, axis=1)
    width_kv = window.shape[1]
    key_win = window[0].reshape(width_kv, KVH, HD)
    value_win = window[1].reshape(width_kv, KVH, HD)
    query_blk = queries.reshape(local_rows, KVH, GROUP, HD)
    scores = jnp.einsum(
        "ighd,jgd->ghij", query_blk, key_win, preferred_element_type=jnp.float32
    ) / math.sqrt(HD)
    positions = jnp.arange(width_kv, dtype=jnp.int32)
    key_local = positions % local_rows
    key_ctx = (ctx_here - (positions // local_rows + 1)) % ctx_count
    query_local = jnp.arange(local_rows, dtype=jnp.int32)[:, None]
    visible = (key_local[None, :] < query_local) | (key_local[None, :] == query_local) & (
        key_ctx[None, :] <= ctx_here
    )
    scores = jnp.where(visible, scores, -jnp.inf)
    lse_prior = prior_lse.reshape(local_rows, KVH, GROUP).transpose(1, 2, 0)
    top_score = jnp.maximum(lse_prior, jnp.max(scores, axis=-1))
    weights = jnp.exp(scores - top_score[..., None])
    prior_weight = jnp.exp(lse_prior - top_score)
    totals = prior_weight + jnp.sum(weights, axis=-1)
    gathered = jnp.einsum(
        "ghij,jgd->ighd",
        weights.astype(jnp.bfloat16),
        value_win,
        preferred_element_type=jnp.float32,
    )
    prior_part = (
        prior_out.reshape(local_rows, KVH, GROUP, HD).astype(jnp.float32)
        * prior_weight.transpose(2, 0, 1)[..., None]
    )
    attended = ((prior_part + gathered) / totals.transpose(2, 0, 1)[..., None]).astype(jnp.bfloat16)
    attended = attended.reshape(local_rows, HEADS * HD)
    model_width = out_proj.shape[1]
    column_half = model_width // 2
    core = ctx_here % 2
    column_rows = lax.all_gather(out_proj, "ctx", axis=0, tiled=True)
    own_half = lax.dynamic_slice_in_dim(column_rows, core * column_half, column_half, axis=1)
    own_half = exchange(own_half[None], False, 0).reshape(-1, column_half)
    other_half = lax.ppermute(own_half, "ctx", [(i, i ^ 1) for i in range(ctx_count)])
    block_rows = out_proj.shape[0]
    attended_perm = (
        attended.reshape(local_rows, ctx_count, ep_count, block_rows)
        .transpose(0, 2, 1, 3)
        .reshape(local_rows, HEADS * HD)
    )
    own_part = jnp.dot(attended_perm, own_half, preferred_element_type=jnp.float32)
    other_part = jnp.dot(attended_perm, other_half, preferred_element_type=jnp.float32)
    projected = jnp.zeros((local_rows, model_width), jnp.float32)
    projected = lax.dynamic_update_slice_in_dim(projected, own_part, core * column_half, axis=1)
    projected = lax.dynamic_update_slice_in_dim(
        projected, other_part, (1 - core) * column_half, axis=1
    )
    mixed_state = (residual.astype(jnp.float32) + projected).astype(jnp.bfloat16)
    state_f = lax.optimization_barrier(mixed_state).astype(jnp.float32)
    normed = (
        state_f * lax.rsqrt(jnp.mean(state_f * state_f, axis=-1, keepdims=True) + 1e-06) * norm_gain
    ).astype(jnp.bfloat16)
    experts_all = ep_count * expert_in.shape[0]
    top_count = expert_ids.shape[1]
    capacity = max(
        local_rows // 4, top_count * ((local_rows + experts_all - 2) // (experts_all - 1))
    )
    flat_ids = expert_ids.reshape(-1)
    one_hot = (flat_ids[:, None] == jnp.arange(experts_all, dtype=jnp.int32)[None, :]).astype(
        jnp.int32
    )
    earlier = jnp.cumsum(one_hot, axis=0) - one_hot
    slot_ids = flat_ids * capacity + jnp.sum(earlier * one_hot, axis=1)
    outgoing = jnp.zeros((experts_all * capacity, model_width), jnp.bfloat16)
    outgoing = (
        outgoing.at[slot_ids]
        .set(jnp.repeat(normed, top_count, axis=0))
        .reshape(experts_all, capacity, model_width)
    )
    weight_in = expert_in[0]
    weight_out = expert_out[0]
    hidden_units = weight_out.shape[0]
    replies = run_expert(
        exchange(outgoing, True, 1),
        weight_in,
        weight_out,
        hidden_units,
    )
    returned = exchange(replies, True, 2)
    picked = returned.reshape(experts_all * capacity, model_width)[slot_ids].reshape(
        local_rows, top_count, model_width
    )
    combined = jnp.sum(route_weight[:, :, None] * picked.astype(jnp.float32), axis=1)
    layer_out = (state_f + combined).astype(jnp.bfloat16)
    return (layer_out, attended)


def solution(mesh):
    return jax.shard_map(
        shards,
        mesh=mesh,
        in_specs=(
            P(("ctx", "ep"), None),
            P(("ctx", "ep"), None),
            P(("ctx", "ep"), None),
            P(("ctx", "ep"), None),
            P(("ctx", "ep"), None),
            P(("ctx", "ep"), None),
            P(("ctx", "ep"), None),
            P(),
            P("ep", None, None),
            P("ep", None, None),
            P(("ctx", "ep"), None),
            P(("ctx", "ep"), None),
        ),
        out_specs=(P(("ctx", "ep"), None), P(("ctx", "ep"), None)),
        check_vma=False,
    )
```

```python
import functools
import math

import jax
import jax.numpy as jnp
from jax import lax
from jax.experimental import pallas as pl
from jax.experimental.pallas import tpu as pltpu
from jax.sharding import PartitionSpec as P

MESH = pl.DeviceIdType.MESH

HEADS = 16
KVH = 2
HD = 128
GROUP = 8


def passed_along(shard, axis, by):
    devices = lax.axis_size(axis)
    return lax.ppermute(shard, axis, [(i, (i + by) % devices) for i in range(devices)])


def exchange_kernel(per_peer, src_ref, dst_ref, send_sem, recv_sem, local_sem):
    n_ep = lax.axis_size("ep")
    n_ctx = lax.axis_size("ctx")
    me = lax.axis_index("ep")
    ctx_me = lax.axis_index("ctx")
    ctx_far = (ctx_me + n_ctx // 2) % n_ctx

    core = ctx_me % 2

    def peer(j):
        p = (me + j + core * (n_ep - 2 * j)) % n_ep
        same = 1 - (p + me) % 2
        return p, same * ctx_me + (1 - same) * ctx_far

    def chunk(p):
        return src_ref.at[p] if per_peer else src_ref.at[0]

    barrier = pltpu.get_barrier_semaphore()

    def greet(j, carry):
        p, c = peer(j)
        pl.semaphore_signal(barrier, inc=1, device_id=(c, p), device_id_type=MESH)
        return carry

    lax.fori_loop(1, n_ep, greet, 0)
    pl.semaphore_wait(barrier, n_ep - 1)

    local = pltpu.make_async_copy(chunk(me), dst_ref.at[me], local_sem)
    local.start()

    def send(j, carry):
        p, c = peer(j)
        pltpu.make_async_remote_copy(
            src_ref=chunk(p),
            dst_ref=dst_ref.at[me],
            send_sem=send_sem.at[p],
            recv_sem=recv_sem.at[me],
            device_id=(c, p),
            device_id_type=MESH,
        ).start()
        return carry

    lax.fori_loop(1, n_ep, send, 0)

    def finish(j, carry):
        p, c = peer(j)
        pltpu.make_async_remote_copy(
            src_ref=chunk(p),
            dst_ref=dst_ref.at[me],
            send_sem=send_sem.at[p],
            recv_sem=recv_sem.at[me],
            device_id=(c, p),
            device_id_type=MESH,
        ).wait_send()
        pltpu.make_async_remote_copy(
            src_ref=chunk(p),
            dst_ref=dst_ref.at[p],
            send_sem=send_sem.at[p],
            recv_sem=recv_sem.at[p],
            device_id=(c, p),
            device_id_type=MESH,
        ).wait_recv()
        return carry

    lax.fori_loop(1, n_ep, finish, 0)
    local.wait()


def exchange(src, per_peer, collective_id):
    n_ep = lax.axis_size("ep")
    block = src.shape[1:]
    moved = n_ep * math.prod(block) * src.dtype.itemsize
    return pl.pallas_call(
        functools.partial(exchange_kernel, per_peer),
        out_shape=jax.ShapeDtypeStruct((n_ep,) + block, src.dtype),
        in_specs=[pl.BlockSpec(memory_space=pl.ANY)],
        out_specs=pl.BlockSpec(memory_space=pl.ANY),
        scratch_shapes=[
            pltpu.SemaphoreType.DMA((n_ep,)),
            pltpu.SemaphoreType.DMA((n_ep,)),
            pltpu.SemaphoreType.DMA,
        ],
        compiler_params=pltpu.CompilerParams(
            collective_id=collective_id, has_side_effects=True
        ),
        cost_estimate=pl.CostEstimate(flops=0, transcendentals=0, bytes_accessed=2 * moved),
    )(src)


def run_expert(inputs, weight_in, weight_out, hidden_units):
    flat_in = inputs.reshape(-1, inputs.shape[-1])
    gate_up = jnp.dot(flat_in, weight_in, preferred_element_type=jnp.float32)
    activated = (jax.nn.silu(gate_up[:, :hidden_units]) * gate_up[:, hidden_units:]).astype(
        jnp.bfloat16
    )
    replies = jnp.dot(activated, weight_out, preferred_element_type=jnp.float32).astype(
        jnp.bfloat16
    )
    return replies.reshape(inputs.shape[:-1] + (weight_out.shape[-1],))


def shards(
    queries,
    keys,
    values,
    prior_out,
    prior_lse,
    residual,
    out_proj,
    norm_gain,
    expert_in,
    expert_out,
    expert_ids,
    route_weight,
):
    local_rows = queries.shape[0]
    ctx_count = lax.axis_size("ctx")
    ctx_here = lax.axis_index("ctx")
    ep_count = lax.axis_size("ep")
    reach_steps = min(2, ctx_count - 1)
    kv_pair = jnp.stack([keys, values])
    arrived = []
    current = kv_pair
    for stride in range(reach_steps):
        current = passed_along(current, "ctx", 1)
        arrived.append(current)
    window = jnp.concatenate(arrived, axis=1)
    width_kv = window.shape[1]
    key_win = window[0].reshape(width_kv, KVH, HD)
    value_win = window[1].reshape(width_kv, KVH, HD)
    query_blk = queries.reshape(local_rows, KVH, GROUP, HD)
    scores = jnp.einsum(
        "ighd,jgd->ghij", query_blk, key_win, preferred_element_type=jnp.float32
    ) / math.sqrt(HD)
    positions = jnp.arange(width_kv, dtype=jnp.int32)
    key_local = positions % local_rows
    key_ctx = (ctx_here - (positions // local_rows + 1)) % ctx_count
    query_local = jnp.arange(local_rows, dtype=jnp.int32)[:, None]
    visible = (key_local[None, :] < query_local) | (key_local[None, :] == query_local) & (
        key_ctx[None, :] <= ctx_here
    )
    scores = jnp.where(visible, scores, -jnp.inf)
    lse_prior = prior_lse.reshape(local_rows, KVH, GROUP).transpose(1, 2, 0)
    top_score = jnp.maximum(lse_prior, jnp.max(scores, axis=-1))
    weights = jnp.exp(scores - top_score[..., None])
    prior_weight = jnp.exp(lse_prior - top_score)
    totals = prior_weight + jnp.sum(weights, axis=-1)
    gathered = jnp.einsum(
        "ghij,jgd->ighd",
        weights.astype(jnp.bfloat16),
        value_win,
        preferred_element_type=jnp.float32,
    )
    prior_part = (
        prior_out.reshape(local_rows, KVH, GROUP, HD).astype(jnp.float32)
        * prior_weight.transpose(2, 0, 1)[..., None]
    )
    attended = ((prior_part + gathered) / totals.transpose(2, 0, 1)[..., None]).astype(jnp.bfloat16)
    attended = attended.reshape(local_rows, HEADS * HD)
    model_width = out_proj.shape[1]
    column_half = model_width // 2
    core = ctx_here % 2
    column_rows = lax.all_gather(out_proj, "ctx", axis=0, tiled=True)
    own_half = lax.dynamic_slice_in_dim(column_rows, core * column_half, column_half, axis=1)
    own_half = exchange(own_half[None], False, 0).reshape(-1, column_half)
    other_half = lax.ppermute(own_half, "ctx", [(i, i ^ 1) for i in range(ctx_count)])
    block_rows = out_proj.shape[0]
    attended_perm = (
        attended.reshape(local_rows, ctx_count, ep_count, block_rows)
        .transpose(0, 2, 1, 3)
        .reshape(local_rows, HEADS * HD)
    )
    own_part = jnp.dot(attended_perm, own_half, preferred_element_type=jnp.float32)
    other_part = jnp.dot(attended_perm, other_half, preferred_element_type=jnp.float32)
    projected = jnp.zeros((local_rows, model_width), jnp.float32)
    projected = lax.dynamic_update_slice_in_dim(projected, own_part, core * column_half, axis=1)
    projected = lax.dynamic_update_slice_in_dim(
        projected, other_part, (1 - core) * column_half, axis=1
    )
    mixed_state = (residual.astype(jnp.float32) + projected).astype(jnp.bfloat16)
    state_f = lax.optimization_barrier(mixed_state).astype(jnp.float32)
    normed = (
        state_f * lax.rsqrt(jnp.mean(state_f * state_f, axis=-1, keepdims=True) + 1e-06) * norm_gain
    ).astype(jnp.bfloat16)
    experts_all = ep_count * expert_in.shape[0]
    top_count = expert_ids.shape[1]
    capacity = max(
        local_rows // 4, top_count * ((local_rows + experts_all - 2) // (experts_all - 1))
    )
    flat_ids = expert_ids.reshape(-1)
    picks = flat_ids.shape[0]
    one_hot = (flat_ids[:, None] == jnp.arange(experts_all, dtype=jnp.int32)[None, :]).astype(
        jnp.bfloat16
    )
    pick_pos = jnp.arange(picks, dtype=jnp.int32)
    before = (pick_pos[None, :] < pick_pos[:, None]).astype(jnp.bfloat16)
    earlier = jnp.dot(before, one_hot, preferred_element_type=jnp.float32)
    rank = jnp.sum(earlier * one_hot.astype(jnp.float32), axis=1).astype(jnp.int32)
    slot_ids = (flat_ids * capacity + rank).reshape(local_rows, top_count)
    slot_pos = jnp.arange(experts_all * capacity, dtype=jnp.int32)
    take = jnp.any(slot_ids[None, :, :] == slot_pos[:, None, None], axis=2).astype(jnp.bfloat16)
    outgoing = (
        jnp.dot(take, normed, preferred_element_type=jnp.float32)
        .astype(jnp.bfloat16)
        .reshape(experts_all, capacity, model_width)
    )
    weight_in = expert_in[0]
    weight_out = expert_out[0]
    hidden_units = weight_out.shape[0]
    replies = run_expert(
        exchange(outgoing, True, 1),
        weight_in,
        weight_out,
        hidden_units,
    )
    returned = exchange(replies, True, 2)
    spread = jnp.sum(
        jnp.where(
            slot_ids[:, :, None] == slot_pos[None, None, :], route_weight[:, :, None], 0.0
        ),
        axis=1,
    )
    combined = jnp.dot(
        spread,
        returned.reshape(experts_all * capacity, model_width).astype(jnp.float32),
        precision=lax.Precision.HIGHEST,
        preferred_element_type=jnp.float32,
    )
    layer_out = (state_f + combined).astype(jnp.bfloat16)
    return (layer_out, attended)


def solution(mesh):
    return jax.shard_map(
        shards,
        mesh=mesh,
        in_specs=(
            P(("ctx", "ep"), None),
            P(("ctx", "ep"), None),
            P(("ctx", "ep"), None),
            P(("ctx", "ep"), None),
            P(("ctx", "ep"), None),
            P(("ctx", "ep"), None),
            P(("ctx", "ep"), None),
            P(),
            P("ep", None, None),
            P("ep", None, None),
            P(("ctx", "ep"), None),
            P(("ctx", "ep"), None),
        ),
        out_specs=(P(("ctx", "ep"), None), P(("ctx", "ep"), None)),
        check_vma=False,
    )
```

```python
import functools
import math

import jax
import jax.numpy as jnp
from jax import lax
from jax.experimental import pallas as pl
from jax.experimental.pallas import tpu as pltpu
from jax.sharding import PartitionSpec as P

MESH = pl.DeviceIdType.MESH

HEADS = 16
KVH = 2
HD = 128
GROUP = 8


def passed_along(shard, axis, by):
    devices = lax.axis_size(axis)
    return lax.ppermute(shard, axis, [(i, (i + by) % devices) for i in range(devices)])


def exchange_kernel(per_peer, src_ref, dst_ref, send_sem, recv_sem, local_sem):
    n_ep = lax.axis_size("ep")
    n_ctx = lax.axis_size("ctx")
    me = lax.axis_index("ep")
    ctx_me = lax.axis_index("ctx")
    ctx_far = (ctx_me + n_ctx // 2) % n_ctx

    core = ctx_me % 2

    def peer(j):
        p = (me + j + core * (n_ep - 2 * j)) % n_ep
        same = 1 - (p + me) % 2
        return p, same * ctx_me + (1 - same) * ctx_far

    def chunk(p):
        return src_ref.at[p] if per_peer else src_ref.at[0]

    barrier = pltpu.get_barrier_semaphore()

    def greet(j, carry):
        p, c = peer(j)
        pl.semaphore_signal(barrier, inc=1, device_id=(c, p), device_id_type=MESH)
        return carry

    lax.fori_loop(1, n_ep, greet, 0)
    pl.semaphore_wait(barrier, n_ep - 1)

    local = pltpu.make_async_copy(chunk(me), dst_ref.at[me], local_sem)
    local.start()

    def send(j, carry):
        p, c = peer(j)
        pltpu.make_async_remote_copy(
            src_ref=chunk(p),
            dst_ref=dst_ref.at[me],
            send_sem=send_sem.at[p],
            recv_sem=recv_sem.at[me],
            device_id=(c, p),
            device_id_type=MESH,
        ).start()
        return carry

    lax.fori_loop(1, n_ep, send, 0)

    def finish(j, carry):
        p, c = peer(j)
        pltpu.make_async_remote_copy(
            src_ref=chunk(p),
            dst_ref=dst_ref.at[me],
            send_sem=send_sem.at[p],
            recv_sem=recv_sem.at[me],
            device_id=(c, p),
            device_id_type=MESH,
        ).wait_send()
        pltpu.make_async_remote_copy(
            src_ref=chunk(p),
            dst_ref=dst_ref.at[p],
            send_sem=send_sem.at[p],
            recv_sem=recv_sem.at[p],
            device_id=(c, p),
            device_id_type=MESH,
        ).wait_recv()
        return carry

    lax.fori_loop(1, n_ep, finish, 0)
    local.wait()


def share_kernel(src_ref, dst_ref, send_sem, recv_sem, local_sem):
    n_ep = lax.axis_size("ep")
    n_ctx = lax.axis_size("ctx")
    half = n_ep // 2
    me = lax.axis_index("ep")
    ctx_me = lax.axis_index("ctx")
    core = ctx_me % 2
    z_near = ctx_me // 2
    z_far = (z_near + n_ctx // 4) % (n_ctx // 2)
    mine = me // half
    owned = 1 - (mine + core) % 2

    def peer(j):
        d = core * half + (me + j) % half
        same = 1 - (d + me) % 2
        z = same * z_near + (1 - same) * z_far
        return d, z * 2 + mine

    def each_remote(body):
        def step(j, carry):
            d, c = peer(j)

            @pl.when(d != me)
            def _():
                body(d, c)

            return carry

        lax.fori_loop(0, half, step, 0)

    barrier = pltpu.get_barrier_semaphore()
    each_remote(
        lambda d, c: pl.semaphore_signal(barrier, inc=1, device_id=(c, d), device_id_type=MESH)
    )
    pl.semaphore_wait(barrier, half - owned)

    @pl.when(owned == 1)
    def _():
        local = pltpu.make_async_copy(src_ref.at[0], dst_ref.at[me % half], local_sem)
        local.start()
        local.wait()

    def copy_to(d, c):
        return pltpu.make_async_remote_copy(
            src_ref=src_ref.at[0],
            dst_ref=dst_ref.at[me % half],
            send_sem=send_sem.at[d % half],
            recv_sem=recv_sem.at[me % half],
            device_id=(c, d),
            device_id_type=MESH,
        )

    def copy_from(d, c):
        return pltpu.make_async_remote_copy(
            src_ref=src_ref.at[0],
            dst_ref=dst_ref.at[d % half],
            send_sem=send_sem.at[d % half],
            recv_sem=recv_sem.at[d % half],
            device_id=(c, d),
            device_id_type=MESH,
        )

    each_remote(lambda d, c: copy_to(d, c).start())
    each_remote(lambda d, c: copy_to(d, c).wait_send())
    each_remote(lambda d, c: copy_from(d, c).wait_recv())


def share(src, collective_id):
    half = lax.axis_size("ep") // 2
    moved = half * math.prod(src.shape) * src.dtype.itemsize
    return pl.pallas_call(
        share_kernel,
        out_shape=jax.ShapeDtypeStruct((half,) + src.shape, src.dtype),
        in_specs=[pl.BlockSpec(memory_space=pl.ANY)],
        out_specs=pl.BlockSpec(memory_space=pl.ANY),
        scratch_shapes=[
            pltpu.SemaphoreType.DMA((half,)),
            pltpu.SemaphoreType.DMA((half,)),
            pltpu.SemaphoreType.DMA,
        ],
        compiler_params=pltpu.CompilerParams(
            collective_id=collective_id, has_side_effects=True
        ),
        cost_estimate=pl.CostEstimate(flops=0, transcendentals=0, bytes_accessed=2 * moved),
    )(src[None])


def exchange(src, per_peer, collective_id):
    n_ep = lax.axis_size("ep")
    block = src.shape[1:]
    moved = n_ep * math.prod(block) * src.dtype.itemsize
    return pl.pallas_call(
        functools.partial(exchange_kernel, per_peer),
        out_shape=jax.ShapeDtypeStruct((n_ep,) + block, src.dtype),
        in_specs=[pl.BlockSpec(memory_space=pl.ANY)],
        out_specs=pl.BlockSpec(memory_space=pl.ANY),
        scratch_shapes=[
            pltpu.SemaphoreType.DMA((n_ep,)),
            pltpu.SemaphoreType.DMA((n_ep,)),
            pltpu.SemaphoreType.DMA,
        ],
        compiler_params=pltpu.CompilerParams(
            collective_id=collective_id, has_side_effects=True
        ),
        cost_estimate=pl.CostEstimate(flops=0, transcendentals=0, bytes_accessed=2 * moved),
    )(src)


def run_expert(inputs, weight_in, weight_out, hidden_units):
    flat_in = inputs.reshape(-1, inputs.shape[-1])
    gate_up = jnp.dot(flat_in, weight_in, preferred_element_type=jnp.float32)
    activated = (jax.nn.silu(gate_up[:, :hidden_units]) * gate_up[:, hidden_units:]).astype(
        jnp.bfloat16
    )
    replies = jnp.dot(activated, weight_out, preferred_element_type=jnp.float32).astype(
        jnp.bfloat16
    )
    return replies.reshape(inputs.shape[:-1] + (weight_out.shape[-1],))


def shards(
    queries,
    keys,
    values,
    prior_out,
    prior_lse,
    residual,
    out_proj,
    norm_gain,
    expert_in,
    expert_out,
    expert_ids,
    route_weight,
):
    local_rows = queries.shape[0]
    ctx_count = lax.axis_size("ctx")
    ctx_here = lax.axis_index("ctx")
    ep_count = lax.axis_size("ep")
    reach_steps = min(2, ctx_count - 1)
    kv_pair = jnp.stack([keys, values])
    arrived = []
    current = kv_pair
    for stride in range(reach_steps):
        current = passed_along(current, "ctx", 1)
        arrived.append(current)
    window = jnp.concatenate(arrived, axis=1)
    width_kv = window.shape[1]
    key_win = window[0].reshape(width_kv, KVH, HD)
    value_win = window[1].reshape(width_kv, KVH, HD)
    query_blk = queries.reshape(local_rows, KVH, GROUP, HD)
    scores = jnp.einsum(
        "ighd,jgd->ghij", query_blk, key_win, preferred_element_type=jnp.float32
    ) / math.sqrt(HD)
    positions = jnp.arange(width_kv, dtype=jnp.int32)
    key_local = positions % local_rows
    key_ctx = (ctx_here - (positions // local_rows + 1)) % ctx_count
    query_local = jnp.arange(local_rows, dtype=jnp.int32)[:, None]
    visible = (key_local[None, :] < query_local) | (key_local[None, :] == query_local) & (
        key_ctx[None, :] <= ctx_here
    )
    scores = jnp.where(visible, scores, -jnp.inf)
    lse_prior = prior_lse.reshape(local_rows, KVH, GROUP).transpose(1, 2, 0)
    top_score = jnp.maximum(lse_prior, jnp.max(scores, axis=-1))
    weights = jnp.exp(scores - top_score[..., None])
    prior_weight = jnp.exp(lse_prior - top_score)
    totals = prior_weight + jnp.sum(weights, axis=-1)
    gathered = jnp.einsum(
        "ghij,jgd->ighd",
        weights.astype(jnp.bfloat16),
        value_win,
        preferred_element_type=jnp.float32,
    )
    prior_part = (
        prior_out.reshape(local_rows, KVH, GROUP, HD).astype(jnp.float32)
        * prior_weight.transpose(2, 0, 1)[..., None]
    )
    attended = ((prior_part + gathered) / totals.transpose(2, 0, 1)[..., None]).astype(jnp.bfloat16)
    attended = attended.reshape(local_rows, HEADS * HD)
    model_width = out_proj.shape[1]
    core = ctx_here % 2
    column_rows = lax.all_gather(out_proj, "ctx", axis=0, tiled=True)
    own_rows = share(column_rows, 0).reshape(-1, model_width)
    other_rows = lax.ppermute(own_rows, "ctx", [(i, i ^ 1) for i in range(ctx_count)])
    block_rows = out_proj.shape[0]
    attended_perm = (
        attended.reshape(local_rows, ctx_count, ep_count, block_rows)
        .transpose(0, 2, 1, 3)
        .reshape(local_rows, HEADS * HD)
    )
    k_half = own_rows.shape[0]
    first, second = attended_perm[:, :k_half], attended_perm[:, k_half:]
    own_cols = jnp.where(core == 0, first, second)
    other_cols = jnp.where(core == 0, second, first)
    projected = jnp.dot(own_cols, own_rows, preferred_element_type=jnp.float32) + jnp.dot(
        other_cols, other_rows, preferred_element_type=jnp.float32
    )
    mixed_state = (residual.astype(jnp.float32) + projected).astype(jnp.bfloat16)
    state_f = lax.optimization_barrier(mixed_state).astype(jnp.float32)
    normed = (
        state_f * lax.rsqrt(jnp.mean(state_f * state_f, axis=-1, keepdims=True) + 1e-06) * norm_gain
    ).astype(jnp.bfloat16)
    experts_all = ep_count * expert_in.shape[0]
    top_count = expert_ids.shape[1]
    capacity = max(
        local_rows // 4, top_count * ((local_rows + experts_all - 2) // (experts_all - 1))
    )
    flat_ids = expert_ids.reshape(-1)
    picks = flat_ids.shape[0]
    one_hot = (flat_ids[:, None] == jnp.arange(experts_all, dtype=jnp.int32)[None, :]).astype(
        jnp.bfloat16
    )
    pick_pos = jnp.arange(picks, dtype=jnp.int32)
    before = (pick_pos[None, :] < pick_pos[:, None]).astype(jnp.bfloat16)
    earlier = jnp.dot(before, one_hot, preferred_element_type=jnp.float32)
    rank = jnp.sum(earlier * one_hot.astype(jnp.float32), axis=1).astype(jnp.int32)
    slot_ids = (flat_ids * capacity + rank).reshape(local_rows, top_count)
    slot_pos = jnp.arange(experts_all * capacity, dtype=jnp.int32)
    take = jnp.any(slot_ids[None, :, :] == slot_pos[:, None, None], axis=2).astype(jnp.bfloat16)
    outgoing = (
        jnp.dot(take, normed, preferred_element_type=jnp.float32)
        .astype(jnp.bfloat16)
        .reshape(experts_all, capacity, model_width)
    )
    weight_in = expert_in[0]
    weight_out = expert_out[0]
    hidden_units = weight_out.shape[0]
    replies = run_expert(
        exchange(outgoing, True, 1),
        weight_in,
        weight_out,
        hidden_units,
    )
    returned = exchange(replies, True, 2)
    spread = jnp.sum(
        jnp.where(
            slot_ids[:, :, None] == slot_pos[None, None, :], route_weight[:, :, None], 0.0
        ),
        axis=1,
    )
    combined = jnp.dot(
        spread,
        returned.reshape(experts_all * capacity, model_width).astype(jnp.float32),
        precision=lax.Precision.HIGHEST,
        preferred_element_type=jnp.float32,
    )
    layer_out = (state_f + combined).astype(jnp.bfloat16)
    return (layer_out, attended)


def solution(mesh):
    return jax.shard_map(
        shards,
        mesh=mesh,
        in_specs=(
            P(("ctx", "ep"), None),
            P(("ctx", "ep"), None),
            P(("ctx", "ep"), None),
            P(("ctx", "ep"), None),
            P(("ctx", "ep"), None),
            P(("ctx", "ep"), None),
            P(("ctx", "ep"), None),
            P(),
            P("ep", None, None),
            P("ep", None, None),
            P(("ctx", "ep"), None),
            P(("ctx", "ep"), None),
        ),
        out_specs=(P(("ctx", "ep"), None), P(("ctx", "ep"), None)),
        check_vma=False,
    )
```

```python
import functools
import math

import jax
import jax.numpy as jnp
from jax import lax
from jax.experimental import pallas as pl
from jax.experimental.pallas import tpu as pltpu
from jax.sharding import PartitionSpec as P

MESH = pl.DeviceIdType.MESH

HEADS = 16
KVH = 2
HD = 128
GROUP = 8


def passed_along(shard, axis, by):
    devices = lax.axis_size(axis)
    return lax.ppermute(shard, axis, [(i, (i + by) % devices) for i in range(devices)])


def exchange_kernel(per_peer, src_ref, dst_ref, send_sem, recv_sem, local_sem):
    n_ep = lax.axis_size("ep")
    n_ctx = lax.axis_size("ctx")
    me = lax.axis_index("ep")
    ctx_me = lax.axis_index("ctx")
    ctx_far = (ctx_me + n_ctx // 2) % n_ctx

    core = ctx_me % 2

    def peer(j):
        p = (me + j + core * (n_ep - 2 * j)) % n_ep
        same = 1 - (p + me) % 2
        return p, same * ctx_me + (1 - same) * ctx_far

    def chunk(p):
        return src_ref.at[p] if per_peer else src_ref.at[0]

    barrier = pltpu.get_barrier_semaphore()

    def greet(j, carry):
        p, c = peer(j)
        pl.semaphore_signal(barrier, inc=1, device_id=(c, p), device_id_type=MESH)
        return carry

    lax.fori_loop(1, n_ep, greet, 0)
    pl.semaphore_wait(barrier, n_ep - 1)

    local = pltpu.make_async_copy(chunk(me), dst_ref.at[me], local_sem)
    local.start()

    def send(j, carry):
        p, c = peer(j)
        pltpu.make_async_remote_copy(
            src_ref=chunk(p),
            dst_ref=dst_ref.at[me],
            send_sem=send_sem.at[p],
            recv_sem=recv_sem.at[me],
            device_id=(c, p),
            device_id_type=MESH,
        ).start()
        return carry

    lax.fori_loop(1, n_ep, send, 0)

    def finish(j, carry):
        p, c = peer(j)
        pltpu.make_async_remote_copy(
            src_ref=chunk(p),
            dst_ref=dst_ref.at[me],
            send_sem=send_sem.at[p],
            recv_sem=recv_sem.at[me],
            device_id=(c, p),
            device_id_type=MESH,
        ).wait_send()
        pltpu.make_async_remote_copy(
            src_ref=chunk(p),
            dst_ref=dst_ref.at[p],
            send_sem=send_sem.at[p],
            recv_sem=recv_sem.at[p],
            device_id=(c, p),
            device_id_type=MESH,
        ).wait_recv()
        return carry

    lax.fori_loop(1, n_ep, finish, 0)
    local.wait()


def share_kernel(src_ref, dst_ref, send_sem, recv_sem, local_sem):
    n_ep = lax.axis_size("ep")
    n_ctx = lax.axis_size("ctx")
    half = n_ep // 2
    me = lax.axis_index("ep")
    ctx_me = lax.axis_index("ctx")
    core = ctx_me % 2
    z_near = ctx_me // 2
    z_far = (z_near + n_ctx // 4) % (n_ctx // 2)
    mine = me // half
    owned = 1 - (mine + core) % 2

    def peer(j):
        d = core * half + (me + j) % half
        same = 1 - (d + me) % 2
        z = same * z_near + (1 - same) * z_far
        return d, z * 2 + mine

    def each_remote(body):
        def step(j, carry):
            d, c = peer(j)

            @pl.when(d != me)
            def _():
                body(d, c)

            return carry

        lax.fori_loop(0, half, step, 0)

    barrier = pltpu.get_barrier_semaphore()
    each_remote(
        lambda d, c: pl.semaphore_signal(barrier, inc=1, device_id=(c, d), device_id_type=MESH)
    )
    pl.semaphore_wait(barrier, half - owned)

    @pl.when(owned == 1)
    def _():
        local = pltpu.make_async_copy(src_ref.at[0], dst_ref.at[me % half], local_sem)
        local.start()
        local.wait()

    def copy_to(d, c):
        return pltpu.make_async_remote_copy(
            src_ref=src_ref.at[0],
            dst_ref=dst_ref.at[me % half],
            send_sem=send_sem.at[d % half],
            recv_sem=recv_sem.at[me % half],
            device_id=(c, d),
            device_id_type=MESH,
        )

    def copy_from(d, c):
        return pltpu.make_async_remote_copy(
            src_ref=src_ref.at[0],
            dst_ref=dst_ref.at[d % half],
            send_sem=send_sem.at[d % half],
            recv_sem=recv_sem.at[d % half],
            device_id=(c, d),
            device_id_type=MESH,
        )

    each_remote(lambda d, c: copy_to(d, c).start())
    each_remote(lambda d, c: copy_to(d, c).wait_send())
    each_remote(lambda d, c: copy_from(d, c).wait_recv())


def share(src, collective_id):
    half = lax.axis_size("ep") // 2
    moved = half * math.prod(src.shape) * src.dtype.itemsize
    return pl.pallas_call(
        share_kernel,
        out_shape=jax.ShapeDtypeStruct((half,) + src.shape, src.dtype),
        in_specs=[pl.BlockSpec(memory_space=pl.ANY)],
        out_specs=pl.BlockSpec(memory_space=pl.ANY),
        scratch_shapes=[
            pltpu.SemaphoreType.DMA((half,)),
            pltpu.SemaphoreType.DMA((half,)),
            pltpu.SemaphoreType.DMA,
        ],
        compiler_params=pltpu.CompilerParams(
            collective_id=collective_id, has_side_effects=True
        ),
        cost_estimate=pl.CostEstimate(flops=0, transcendentals=0, bytes_accessed=2 * moved),
    )(src[None])


def exchange(src, per_peer, collective_id):
    n_ep = lax.axis_size("ep")
    block = src.shape[1:]
    moved = n_ep * math.prod(block) * src.dtype.itemsize
    return pl.pallas_call(
        functools.partial(exchange_kernel, per_peer),
        out_shape=jax.ShapeDtypeStruct((n_ep,) + block, src.dtype),
        in_specs=[pl.BlockSpec(memory_space=pl.ANY)],
        out_specs=pl.BlockSpec(memory_space=pl.ANY),
        scratch_shapes=[
            pltpu.SemaphoreType.DMA((n_ep,)),
            pltpu.SemaphoreType.DMA((n_ep,)),
            pltpu.SemaphoreType.DMA,
        ],
        compiler_params=pltpu.CompilerParams(
            collective_id=collective_id, has_side_effects=True
        ),
        cost_estimate=pl.CostEstimate(flops=0, transcendentals=0, bytes_accessed=2 * moved),
    )(src)


def run_expert(inputs, weight_in, weight_out, hidden_units):
    flat_in = inputs.reshape(-1, inputs.shape[-1])
    gate_up = jnp.dot(flat_in, weight_in, preferred_element_type=jnp.float32)
    activated = (jax.nn.silu(gate_up[:, :hidden_units]) * gate_up[:, hidden_units:]).astype(
        jnp.bfloat16
    )
    replies = jnp.dot(activated, weight_out, preferred_element_type=jnp.float32).astype(
        jnp.bfloat16
    )
    return replies.reshape(inputs.shape[:-1] + (weight_out.shape[-1],))


def shards(
    queries,
    keys,
    values,
    prior_out,
    prior_lse,
    residual,
    out_proj,
    norm_gain,
    expert_in,
    expert_out,
    expert_ids,
    route_weight,
):
    local_rows = queries.shape[0]
    ctx_count = lax.axis_size("ctx")
    ctx_here = lax.axis_index("ctx")
    ep_count = lax.axis_size("ep")
    reach_steps = min(2, ctx_count - 1)
    kv_pair = jnp.stack([keys, values])
    arrived = []
    current = kv_pair
    for stride in range(reach_steps):
        current = passed_along(current, "ctx", 1)
        arrived.append(current)
    window = jnp.concatenate(arrived, axis=1)
    width_kv = window.shape[1]
    key_win = window[0].reshape(width_kv, KVH, HD)
    value_win = window[1].reshape(width_kv, KVH, HD)
    query_blk = queries.reshape(local_rows, KVH, GROUP, HD)
    scores = jnp.einsum(
        "ighd,jgd->ghij", query_blk, key_win, preferred_element_type=jnp.float32
    ) / math.sqrt(HD)
    positions = jnp.arange(width_kv, dtype=jnp.int32)
    key_local = positions % local_rows
    key_ctx = (ctx_here - (positions // local_rows + 1)) % ctx_count
    query_local = jnp.arange(local_rows, dtype=jnp.int32)[:, None]
    visible = (key_local[None, :] < query_local) | (key_local[None, :] == query_local) & (
        key_ctx[None, :] <= ctx_here
    )
    scores = jnp.where(visible, scores, -jnp.inf)
    lse_prior = prior_lse.reshape(local_rows, KVH, GROUP).transpose(1, 2, 0)
    top_score = jnp.maximum(lse_prior, jnp.max(scores, axis=-1))
    weights = jnp.exp(scores - top_score[..., None])
    prior_weight = jnp.exp(lse_prior - top_score)
    totals = prior_weight + jnp.sum(weights, axis=-1)
    gathered = jnp.einsum(
        "ghij,jgd->ighd",
        weights.astype(jnp.bfloat16),
        value_win,
        preferred_element_type=jnp.float32,
    )
    prior_part = (
        prior_out.reshape(local_rows, KVH, GROUP, HD).astype(jnp.float32)
        * prior_weight.transpose(2, 0, 1)[..., None]
    )
    attended = ((prior_part + gathered) / totals.transpose(2, 0, 1)[..., None]).astype(jnp.bfloat16)
    attended = attended.reshape(local_rows, HEADS * HD)
    model_width = out_proj.shape[1]
    core = ctx_here % 2
    column_rows = lax.all_gather(out_proj, "ctx", axis=0, tiled=True)
    kernel_cols = model_width // 2
    quarter = (model_width - kernel_cols) // 2
    side_rows = lax.dynamic_slice_in_dim(column_rows, kernel_cols + core * quarter, quarter, axis=1)
    side_rows = lax.all_gather(side_rows, "ep", axis=0, tiled=True)
    own_rows = share(column_rows[:, :kernel_cols], 0).reshape(-1, kernel_cols)
    swap = [(i, i ^ 1) for i in range(ctx_count)]
    other_rows = lax.ppermute(own_rows, "ctx", swap)
    other_side = lax.ppermute(side_rows, "ctx", swap)
    block_rows = out_proj.shape[0]
    attended_perm = (
        attended.reshape(local_rows, ctx_count, ep_count, block_rows)
        .transpose(0, 2, 1, 3)
        .reshape(local_rows, HEADS * HD)
    )
    k_half = own_rows.shape[0]
    first, second = attended_perm[:, :k_half], attended_perm[:, k_half:]
    own_k = jnp.where(core == 0, first, second)
    other_k = jnp.where(core == 0, second, first)
    kernel_part = jnp.dot(own_k, own_rows, preferred_element_type=jnp.float32) + jnp.dot(
        other_k, other_rows, preferred_element_type=jnp.float32
    )
    own_side = jnp.dot(attended_perm, side_rows, preferred_element_type=jnp.float32)
    far_side = jnp.dot(attended_perm, other_side, preferred_element_type=jnp.float32)
    projected = jnp.zeros((local_rows, model_width), jnp.float32)
    projected = lax.dynamic_update_slice_in_dim(projected, kernel_part, 0, axis=1)
    projected = lax.dynamic_update_slice_in_dim(
        projected, own_side, kernel_cols + core * quarter, axis=1
    )
    projected = lax.dynamic_update_slice_in_dim(
        projected, far_side, kernel_cols + (1 - core) * quarter, axis=1
    )
    mixed_state = (residual.astype(jnp.float32) + projected).astype(jnp.bfloat16)
    state_f = lax.optimization_barrier(mixed_state).astype(jnp.float32)
    normed = (
        state_f * lax.rsqrt(jnp.mean(state_f * state_f, axis=-1, keepdims=True) + 1e-06) * norm_gain
    ).astype(jnp.bfloat16)
    experts_all = ep_count * expert_in.shape[0]
    top_count = expert_ids.shape[1]
    capacity = max(
        local_rows // 4, top_count * ((local_rows + experts_all - 2) // (experts_all - 1))
    )
    flat_ids = expert_ids.reshape(-1)
    picks = flat_ids.shape[0]
    one_hot = (flat_ids[:, None] == jnp.arange(experts_all, dtype=jnp.int32)[None, :]).astype(
        jnp.bfloat16
    )
    pick_pos = jnp.arange(picks, dtype=jnp.int32)
    before = (pick_pos[None, :] < pick_pos[:, None]).astype(jnp.bfloat16)
    earlier = jnp.dot(before, one_hot, preferred_element_type=jnp.float32)
    rank = jnp.sum(earlier * one_hot.astype(jnp.float32), axis=1).astype(jnp.int32)
    slot_ids = (flat_ids * capacity + rank).reshape(local_rows, top_count)
    slot_pos = jnp.arange(experts_all * capacity, dtype=jnp.int32)
    take = jnp.any(slot_ids[None, :, :] == slot_pos[:, None, None], axis=2).astype(jnp.bfloat16)
    outgoing = (
        jnp.dot(take, normed, preferred_element_type=jnp.float32)
        .astype(jnp.bfloat16)
        .reshape(experts_all, capacity, model_width)
    )
    weight_in = expert_in[0]
    weight_out = expert_out[0]
    hidden_units = weight_out.shape[0]
    replies = run_expert(
        exchange(outgoing, True, 1),
        weight_in,
        weight_out,
        hidden_units,
    )
    returned = exchange(replies, True, 2)
    spread = jnp.sum(
        jnp.where(
            slot_ids[:, :, None] == slot_pos[None, None, :], route_weight[:, :, None], 0.0
        ),
        axis=1,
    )
    combined = jnp.dot(
        spread,
        returned.reshape(experts_all * capacity, model_width).astype(jnp.float32),
        precision=lax.Precision.HIGHEST,
        preferred_element_type=jnp.float32,
    )
    layer_out = (state_f + combined).astype(jnp.bfloat16)
    return (layer_out, attended)


def solution(mesh):
    return jax.shard_map(
        shards,
        mesh=mesh,
        in_specs=(
            P(("ctx", "ep"), None),
            P(("ctx", "ep"), None),
            P(("ctx", "ep"), None),
            P(("ctx", "ep"), None),
            P(("ctx", "ep"), None),
            P(("ctx", "ep"), None),
            P(("ctx", "ep"), None),
            P(),
            P("ep", None, None),
            P("ep", None, None),
            P(("ctx", "ep"), None),
            P(("ctx", "ep"), None),
        ),
        out_specs=(P(("ctx", "ep"), None), P(("ctx", "ep"), None)),
        check_vma=False,
    )
```

```python
import functools
import math

import jax
import jax.numpy as jnp
from jax import lax
from jax.experimental import pallas as pl
from jax.experimental.pallas import tpu as pltpu
from jax.sharding import PartitionSpec as P

MESH = pl.DeviceIdType.MESH

HEADS = 16
KVH = 2
HD = 128
GROUP = 8


def passed_along(shard, axis, by):
    devices = lax.axis_size(axis)
    return lax.ppermute(shard, axis, [(i, (i + by) % devices) for i in range(devices)])


def exchange_kernel(per_peer, src_ref, dst_ref, send_sem, recv_sem, local_sem):
    n_ep = lax.axis_size("ep")
    n_ctx = lax.axis_size("ctx")
    me = lax.axis_index("ep")
    ctx_me = lax.axis_index("ctx")
    ctx_far = (ctx_me + n_ctx // 2) % n_ctx

    core = ctx_me % 2

    def peer(j):
        p = (me + j + core * (n_ep - 2 * j)) % n_ep
        same = 1 - (p + me) % 2
        return p, same * ctx_me + (1 - same) * ctx_far

    def chunk(p):
        return src_ref.at[p] if per_peer else src_ref.at[0]

    barrier = pltpu.get_barrier_semaphore()

    def greet(j, carry):
        p, c = peer(j)
        pl.semaphore_signal(barrier, inc=1, device_id=(c, p), device_id_type=MESH)
        return carry

    lax.fori_loop(1, n_ep, greet, 0)
    pl.semaphore_wait(barrier, n_ep - 1)

    local = pltpu.make_async_copy(chunk(me), dst_ref.at[me], local_sem)
    local.start()

    def send(j, carry):
        p, c = peer(j)
        pltpu.make_async_remote_copy(
            src_ref=chunk(p),
            dst_ref=dst_ref.at[me],
            send_sem=send_sem.at[p],
            recv_sem=recv_sem.at[me],
            device_id=(c, p),
            device_id_type=MESH,
        ).start()
        return carry

    lax.fori_loop(1, n_ep, send, 0)

    def finish(j, carry):
        p, c = peer(j)
        pltpu.make_async_remote_copy(
            src_ref=chunk(p),
            dst_ref=dst_ref.at[me],
            send_sem=send_sem.at[p],
            recv_sem=recv_sem.at[me],
            device_id=(c, p),
            device_id_type=MESH,
        ).wait_send()
        pltpu.make_async_remote_copy(
            src_ref=chunk(p),
            dst_ref=dst_ref.at[p],
            send_sem=send_sem.at[p],
            recv_sem=recv_sem.at[p],
            device_id=(c, p),
            device_id_type=MESH,
        ).wait_recv()
        return carry

    lax.fori_loop(1, n_ep, finish, 0)
    local.wait()


def exchange(src, per_peer, collective_id):
    n_ep = lax.axis_size("ep")
    block = src.shape[1:]
    moved = n_ep * math.prod(block) * src.dtype.itemsize
    return pl.pallas_call(
        functools.partial(exchange_kernel, per_peer),
        out_shape=jax.ShapeDtypeStruct((n_ep,) + block, src.dtype),
        in_specs=[pl.BlockSpec(memory_space=pl.ANY)],
        out_specs=pl.BlockSpec(memory_space=pl.ANY),
        scratch_shapes=[
            pltpu.SemaphoreType.DMA((n_ep,)),
            pltpu.SemaphoreType.DMA((n_ep,)),
            pltpu.SemaphoreType.DMA,
        ],
        compiler_params=pltpu.CompilerParams(
            collective_id=collective_id, has_side_effects=True
        ),
        cost_estimate=pl.CostEstimate(flops=0, transcendentals=0, bytes_accessed=2 * moved),
    )(src)


def run_expert(inputs, weight_in, weight_out, hidden_units):
    flat_in = inputs.reshape(-1, inputs.shape[-1])
    gate_up = jnp.dot(flat_in, weight_in, preferred_element_type=jnp.float32)
    activated = (jax.nn.silu(gate_up[:, :hidden_units]) * gate_up[:, hidden_units:]).astype(
        jnp.bfloat16
    )
    replies = jnp.dot(activated, weight_out, preferred_element_type=jnp.float32).astype(
        jnp.bfloat16
    )
    return replies.reshape(inputs.shape[:-1] + (weight_out.shape[-1],))


def shards(
    queries,
    keys,
    values,
    prior_out,
    prior_lse,
    residual,
    out_proj,
    norm_gain,
    expert_in,
    expert_out,
    expert_ids,
    route_weight,
):
    local_rows = queries.shape[0]
    ctx_count = lax.axis_size("ctx")
    ctx_here = lax.axis_index("ctx")
    ep_count = lax.axis_size("ep")
    reach_steps = min(2, ctx_count - 1)
    kv_pair = jnp.stack([keys, values])
    arrived = []
    current = kv_pair
    for stride in range(reach_steps):
        current = passed_along(current, "ctx", 1)
        arrived.append(current)
    window = jnp.concatenate(arrived, axis=1)
    width_kv = window.shape[1]
    key_win = window[0].reshape(width_kv, KVH, HD)
    value_win = window[1].reshape(width_kv, KVH, HD)
    query_blk = queries.reshape(local_rows, KVH, GROUP, HD)
    scores = jnp.einsum(
        "ighd,jgd->ghij", query_blk, key_win, preferred_element_type=jnp.float32
    ) / math.sqrt(HD)
    positions = jnp.arange(width_kv, dtype=jnp.int32)
    key_local = positions % local_rows
    key_ctx = (ctx_here - (positions // local_rows + 1)) % ctx_count
    query_local = jnp.arange(local_rows, dtype=jnp.int32)[:, None]
    visible = (key_local[None, :] < query_local) | (key_local[None, :] == query_local) & (
        key_ctx[None, :] <= ctx_here
    )
    scores = jnp.where(visible, scores, -jnp.inf)
    lse_prior = prior_lse.reshape(local_rows, KVH, GROUP).transpose(1, 2, 0)
    top_score = jnp.maximum(lse_prior, jnp.max(scores, axis=-1))
    weights = jnp.exp(scores - top_score[..., None])
    prior_weight = jnp.exp(lse_prior - top_score)
    totals = prior_weight + jnp.sum(weights, axis=-1)
    gathered = jnp.einsum(
        "ghij,jgd->ighd",
        weights.astype(jnp.bfloat16),
        value_win,
        preferred_element_type=jnp.float32,
    )
    prior_part = (
        prior_out.reshape(local_rows, KVH, GROUP, HD).astype(jnp.float32)
        * prior_weight.transpose(2, 0, 1)[..., None]
    )
    attended = ((prior_part + gathered) / totals.transpose(2, 0, 1)[..., None]).astype(jnp.bfloat16)
    attended = attended.reshape(local_rows, HEADS * HD)
    model_width = out_proj.shape[1]
    column_half = model_width // 2
    core = ctx_here % 2
    column_rows = lax.all_gather(out_proj, "ctx", axis=0, tiled=True)
    own_half = lax.dynamic_slice_in_dim(column_rows, core * column_half, column_half, axis=1)
    own_half = exchange(own_half[None], False, 0).reshape(-1, column_half)
    other_half = lax.ppermute(own_half, "ctx", [(i, i ^ 1) for i in range(ctx_count)])
    block_rows = out_proj.shape[0]
    attended_perm = (
        attended.reshape(local_rows, ctx_count, ep_count, block_rows)
        .transpose(0, 2, 1, 3)
        .reshape(local_rows, HEADS * HD)
    )
    own_part = jnp.dot(attended_perm, own_half, preferred_element_type=jnp.float32)
    other_part = jnp.dot(attended_perm, other_half, preferred_element_type=jnp.float32)
    projected = jnp.zeros((local_rows, model_width), jnp.float32)
    projected = lax.dynamic_update_slice_in_dim(projected, own_part, core * column_half, axis=1)
    projected = lax.dynamic_update_slice_in_dim(
        projected, other_part, (1 - core) * column_half, axis=1
    )
    mixed_state = (residual.astype(jnp.float32) + projected).astype(jnp.bfloat16)
    state_f = lax.optimization_barrier(mixed_state).astype(jnp.float32)
    normed = (
        state_f * lax.rsqrt(jnp.mean(state_f * state_f, axis=-1, keepdims=True) + 1e-06) * norm_gain
    ).astype(jnp.bfloat16)
    experts_all = ep_count * expert_in.shape[0]
    top_count = expert_ids.shape[1]
    capacity = max(
        local_rows // 4, top_count * ((local_rows + experts_all - 2) // (experts_all - 1))
    )
    flat_ids = expert_ids.reshape(-1)
    picks = flat_ids.shape[0]
    one_hot = (flat_ids[:, None] == jnp.arange(experts_all, dtype=jnp.int32)[None, :]).astype(
        jnp.bfloat16
    )
    pick_pos = jnp.arange(picks, dtype=jnp.int32)
    before = (pick_pos[None, :] < pick_pos[:, None]).astype(jnp.bfloat16)
    earlier = jnp.dot(before, one_hot, preferred_element_type=jnp.float32)
    rank = jnp.sum(earlier * one_hot.astype(jnp.float32), axis=1).astype(jnp.int32)
    slot_ids = (flat_ids * capacity + rank).reshape(local_rows, top_count)
    slot_pos = jnp.arange(experts_all * capacity, dtype=jnp.int32)
    take = jnp.any(slot_ids[None, :, :] == slot_pos[:, None, None], axis=2).astype(jnp.bfloat16)
    lanes = 128
    chunk_rows = capacity * model_width // lanes
    outgoing = (
        jnp.dot(take, normed, preferred_element_type=jnp.float32)
        .astype(jnp.bfloat16)
        .reshape(experts_all, chunk_rows, lanes)
    )
    weight_in = expert_in[0]
    weight_out = expert_out[0]
    hidden_units = weight_out.shape[0]
    replies = run_expert(
        exchange(outgoing, True, 1).reshape(experts_all, capacity, model_width),
        weight_in,
        weight_out,
        hidden_units,
    )
    returned = exchange(replies.reshape(experts_all, chunk_rows, lanes), True, 2)
    spread = jnp.sum(
        jnp.where(
            slot_ids[:, :, None] == slot_pos[None, None, :], route_weight[:, :, None], 0.0
        ),
        axis=1,
    )
    combined = jnp.dot(
        spread,
        returned.reshape(experts_all * capacity, model_width).astype(jnp.float32),
        precision=lax.Precision.HIGHEST,
        preferred_element_type=jnp.float32,
    )
    layer_out = (state_f + combined).astype(jnp.bfloat16)
    return (layer_out, attended)


def solution(mesh):
    return jax.shard_map(
        shards,
        mesh=mesh,
        in_specs=(
            P(("ctx", "ep"), None),
            P(("ctx", "ep"), None),
            P(("ctx", "ep"), None),
            P(("ctx", "ep"), None),
            P(("ctx", "ep"), None),
            P(("ctx", "ep"), None),
            P(("ctx", "ep"), None),
            P(),
            P("ep", None, None),
            P("ep", None, None),
            P(("ctx", "ep"), None),
            P(("ctx", "ep"), None),
        ),
        out_specs=(P(("ctx", "ep"), None), P(("ctx", "ep"), None)),
        check_vma=False,
    )
```

```python
import functools
import math

import jax
import jax.numpy as jnp
from jax import lax
from jax.experimental import pallas as pl
from jax.experimental.pallas import tpu as pltpu
from jax.sharding import PartitionSpec as P

MESH = pl.DeviceIdType.MESH

HEADS = 16
KVH = 2
HD = 128
GROUP = 8


def passed_along(shard, axis, by):
    devices = lax.axis_size(axis)
    return lax.ppermute(shard, axis, [(i, (i + by) % devices) for i in range(devices)])


def exchange_kernel(per_peer, src_ref, dst_ref, send_sem, recv_sem, local_sem):
    n_ep = lax.axis_size("ep")
    n_ctx = lax.axis_size("ctx")
    me = lax.axis_index("ep")
    ctx_me = lax.axis_index("ctx")
    ctx_far = (ctx_me + n_ctx // 2) % n_ctx

    core = ctx_me % 2

    def peer(j):
        p = (me + j + core * (n_ep - 2 * j)) % n_ep
        same = 1 - (p + me) % 2
        return p, same * ctx_me + (1 - same) * ctx_far

    def chunk(p):
        return src_ref.at[p] if per_peer else src_ref.at[0]

    barrier = pltpu.get_barrier_semaphore()

    def greet(j, carry):
        p, c = peer(j)
        pl.semaphore_signal(barrier, inc=1, device_id=(c, p), device_id_type=MESH)
        return carry

    lax.fori_loop(1, n_ep, greet, 0)
    pl.semaphore_wait(barrier, n_ep - 1)

    local = pltpu.make_async_copy(chunk(me), dst_ref.at[me], local_sem)
    local.start()

    def send(j, carry):
        p, c = peer(j)
        pltpu.make_async_remote_copy(
            src_ref=chunk(p),
            dst_ref=dst_ref.at[me],
            send_sem=send_sem.at[p],
            recv_sem=recv_sem.at[me],
            device_id=(c, p),
            device_id_type=MESH,
        ).start()
        return carry

    lax.fori_loop(1, n_ep, send, 0)

    def finish(j, carry):
        p, c = peer(j)
        pltpu.make_async_remote_copy(
            src_ref=chunk(p),
            dst_ref=dst_ref.at[me],
            send_sem=send_sem.at[p],
            recv_sem=recv_sem.at[me],
            device_id=(c, p),
            device_id_type=MESH,
        ).wait_send()
        pltpu.make_async_remote_copy(
            src_ref=chunk(p),
            dst_ref=dst_ref.at[p],
            send_sem=send_sem.at[p],
            recv_sem=recv_sem.at[p],
            device_id=(c, p),
            device_id_type=MESH,
        ).wait_recv()
        return carry

    lax.fori_loop(1, n_ep, finish, 0)
    local.wait()


def exchange(src, per_peer, collective_id):
    n_ep = lax.axis_size("ep")
    block = src.shape[1:]
    moved = n_ep * math.prod(block) * src.dtype.itemsize
    return pl.pallas_call(
        functools.partial(exchange_kernel, per_peer),
        out_shape=jax.ShapeDtypeStruct((n_ep,) + block, src.dtype),
        in_specs=[pl.BlockSpec(memory_space=pl.ANY)],
        out_specs=pl.BlockSpec(memory_space=pl.ANY),
        scratch_shapes=[
            pltpu.SemaphoreType.DMA((n_ep,)),
            pltpu.SemaphoreType.DMA((n_ep,)),
            pltpu.SemaphoreType.DMA,
        ],
        compiler_params=pltpu.CompilerParams(
            collective_id=collective_id, has_side_effects=True
        ),
        cost_estimate=pl.CostEstimate(flops=0, transcendentals=0, bytes_accessed=2 * moved),
    )(src)


def run_expert(inputs, weight_in, weight_out, hidden_units):
    flat_in = inputs.reshape(-1, inputs.shape[-1])
    gate_up = jnp.dot(flat_in, weight_in, preferred_element_type=jnp.float32)
    activated = (jax.nn.silu(gate_up[:, :hidden_units]) * gate_up[:, hidden_units:]).astype(
        jnp.bfloat16
    )
    replies = jnp.dot(activated, weight_out, preferred_element_type=jnp.float32).astype(
        jnp.bfloat16
    )
    return replies.reshape(inputs.shape[:-1] + (weight_out.shape[-1],))


def shards(
    queries,
    keys,
    values,
    prior_out,
    prior_lse,
    residual,
    out_proj,
    norm_gain,
    expert_in,
    expert_out,
    expert_ids,
    route_weight,
):
    local_rows = queries.shape[0]
    ctx_count = lax.axis_size("ctx")
    ctx_here = lax.axis_index("ctx")
    ep_count = lax.axis_size("ep")
    reach_steps = min(2, ctx_count - 1)
    kv_pair = jnp.stack([keys, values])
    arrived = []
    current = kv_pair
    for stride in range(reach_steps):
        current = passed_along(current, "ctx", 1)
        arrived.append(current)
    window = jnp.concatenate(arrived, axis=1)
    width_kv = window.shape[1]
    key_win = window[0].reshape(width_kv, KVH, HD)
    value_win = window[1].reshape(width_kv, KVH, HD)
    query_blk = queries.reshape(local_rows, KVH, GROUP, HD)
    scores = jnp.einsum(
        "ighd,jgd->ghij", query_blk, key_win, preferred_element_type=jnp.float32
    ) / math.sqrt(HD)
    positions = jnp.arange(width_kv, dtype=jnp.int32)
    key_local = positions % local_rows
    key_ctx = (ctx_here - (positions // local_rows + 1)) % ctx_count
    query_local = jnp.arange(local_rows, dtype=jnp.int32)[:, None]
    visible = (key_local[None, :] < query_local) | (key_local[None, :] == query_local) & (
        key_ctx[None, :] <= ctx_here
    )
    scores = jnp.where(visible, scores, -jnp.inf)
    lse_prior = prior_lse.reshape(local_rows, KVH, GROUP).transpose(1, 2, 0)
    top_score = jnp.maximum(lse_prior, jnp.max(scores, axis=-1))
    weights = jnp.exp(scores - top_score[..., None])
    prior_weight = jnp.exp(lse_prior - top_score)
    totals = prior_weight + jnp.sum(weights, axis=-1)
    gathered = jnp.einsum(
        "ghij,jgd->ighd",
        weights.astype(jnp.bfloat16),
        value_win,
        preferred_element_type=jnp.float32,
    )
    prior_part = (
        prior_out.reshape(local_rows, KVH, GROUP, HD).astype(jnp.float32)
        * prior_weight.transpose(2, 0, 1)[..., None]
    )
    attended = ((prior_part + gathered) / totals.transpose(2, 0, 1)[..., None]).astype(jnp.bfloat16)
    attended = attended.reshape(local_rows, HEADS * HD)
    model_width = out_proj.shape[1]
    column_half = model_width // 2
    core = ctx_here % 2
    block_count = out_proj.shape[0]
    column_rows = jnp.zeros((ctx_count * block_count, model_width), out_proj.dtype)
    column_rows = lax.dynamic_update_slice_in_dim(
        column_rows, out_proj, ctx_here * block_count, axis=0
    )
    column_rows = lax.psum(column_rows, "ctx")
    own_half = lax.dynamic_slice_in_dim(column_rows, core * column_half, column_half, axis=1)
    own_half, attended = lax.optimization_barrier((own_half, attended))
    own_half = exchange(own_half[None], False, 0).reshape(-1, column_half)
    other_half = lax.ppermute(own_half, "ctx", [(i, i ^ 1) for i in range(ctx_count)])
    block_rows = out_proj.shape[0]
    attended_perm = (
        attended.reshape(local_rows, ctx_count, ep_count, block_rows)
        .transpose(0, 2, 1, 3)
        .reshape(local_rows, HEADS * HD)
    )
    own_part = jnp.dot(attended_perm, own_half, preferred_element_type=jnp.float32)
    other_part = jnp.dot(attended_perm, other_half, preferred_element_type=jnp.float32)
    projected = jnp.zeros((local_rows, model_width), jnp.float32)
    projected = lax.dynamic_update_slice_in_dim(projected, own_part, core * column_half, axis=1)
    projected = lax.dynamic_update_slice_in_dim(
        projected, other_part, (1 - core) * column_half, axis=1
    )
    mixed_state = (residual.astype(jnp.float32) + projected).astype(jnp.bfloat16)
    state_f = lax.optimization_barrier(mixed_state).astype(jnp.float32)
    normed = (
        state_f * lax.rsqrt(jnp.mean(state_f * state_f, axis=-1, keepdims=True) + 1e-06) * norm_gain
    ).astype(jnp.bfloat16)
    experts_all = ep_count * expert_in.shape[0]
    top_count = expert_ids.shape[1]
    capacity = max(
        local_rows // 4, top_count * ((local_rows + experts_all - 2) // (experts_all - 1))
    )
    flat_ids = expert_ids.reshape(-1)
    picks = flat_ids.shape[0]
    one_hot = (flat_ids[:, None] == jnp.arange(experts_all, dtype=jnp.int32)[None, :]).astype(
        jnp.bfloat16
    )
    pick_pos = jnp.arange(picks, dtype=jnp.int32)
    before = (pick_pos[None, :] < pick_pos[:, None]).astype(jnp.bfloat16)
    earlier = jnp.dot(before, one_hot, preferred_element_type=jnp.float32)
    rank = jnp.sum(earlier * one_hot.astype(jnp.float32), axis=1).astype(jnp.int32)
    slot_ids = (flat_ids * capacity + rank).reshape(local_rows, top_count)
    slot_pos = jnp.arange(experts_all * capacity, dtype=jnp.int32)
    take = jnp.any(slot_ids[None, :, :] == slot_pos[:, None, None], axis=2).astype(jnp.bfloat16)
    outgoing = (
        jnp.dot(take, normed, preferred_element_type=jnp.float32)
        .astype(jnp.bfloat16)
        .reshape(experts_all, capacity, model_width)
    )
    weight_in = expert_in[0]
    weight_out = expert_out[0]
    hidden_units = weight_out.shape[0]
    replies = run_expert(
        exchange(outgoing, True, 1),
        weight_in,
        weight_out,
        hidden_units,
    )
    returned = exchange(replies, True, 2)
    spread = jnp.sum(
        jnp.where(
            slot_ids[:, :, None] == slot_pos[None, None, :], route_weight[:, :, None], 0.0
        ),
        axis=1,
    )
    combined = jnp.dot(
        spread,
        returned.reshape(experts_all * capacity, model_width).astype(jnp.float32),
        precision=lax.Precision.HIGHEST,
        preferred_element_type=jnp.float32,
    )
    layer_out = (state_f + combined).astype(jnp.bfloat16)
    return (layer_out, attended)


def solution(mesh):
    return jax.shard_map(
        shards,
        mesh=mesh,
        in_specs=(
            P(("ctx", "ep"), None),
            P(("ctx", "ep"), None),
            P(("ctx", "ep"), None),
            P(("ctx", "ep"), None),
            P(("ctx", "ep"), None),
            P(("ctx", "ep"), None),
            P(("ctx", "ep"), None),
            P(),
            P("ep", None, None),
            P("ep", None, None),
            P(("ctx", "ep"), None),
            P(("ctx", "ep"), None),
        ),
        out_specs=(P(("ctx", "ep"), None), P(("ctx", "ep"), None)),
        check_vma=False,
    )
```

```python
import functools
import math

import jax
import jax.numpy as jnp
from jax import lax
from jax.experimental import pallas as pl
from jax.experimental.pallas import tpu as pltpu
from jax.sharding import PartitionSpec as P

MESH = pl.DeviceIdType.MESH

HEADS = 16
KVH = 2
HD = 128
GROUP = 8


def passed_along(shard, axis, by):
    devices = lax.axis_size(axis)
    return lax.ppermute(shard, axis, [(i, (i + by) % devices) for i in range(devices)])


def exchange_kernel(per_peer, src_ref, dst_ref, send_sem, recv_sem, local_sem):
    n_ep = lax.axis_size("ep")
    n_ctx = lax.axis_size("ctx")
    me = lax.axis_index("ep")
    ctx_me = lax.axis_index("ctx")
    ctx_far = (ctx_me + n_ctx // 2) % n_ctx

    core = ctx_me % 2

    bits = max(n_ep - 1, 1).bit_length()

    def peer(j):
        step = j + core * (n_ep - 2 * j)
        p = 0
        for b in range(bits):
            p = p + ((me // 2**b + step // 2**b) % 2) * 2**b
        same = 1 - (p + me) % 2
        return p, same * ctx_me + (1 - same) * ctx_far

    def chunk(p):
        return src_ref.at[p] if per_peer else src_ref.at[0]

    barrier = pltpu.get_barrier_semaphore()

    def greet(j, carry):
        p, c = peer(j)
        pl.semaphore_signal(barrier, inc=1, device_id=(c, p), device_id_type=MESH)
        return carry

    lax.fori_loop(1, n_ep, greet, 0)
    pl.semaphore_wait(barrier, n_ep - 1)

    local = pltpu.make_async_copy(chunk(me), dst_ref.at[me], local_sem)
    local.start()

    def send(j, carry):
        p, c = peer(j)
        pltpu.make_async_remote_copy(
            src_ref=chunk(p),
            dst_ref=dst_ref.at[me],
            send_sem=send_sem.at[p],
            recv_sem=recv_sem.at[me],
            device_id=(c, p),
            device_id_type=MESH,
        ).start()
        return carry

    lax.fori_loop(1, n_ep, send, 0)

    def finish(j, carry):
        p, c = peer(j)
        pltpu.make_async_remote_copy(
            src_ref=chunk(p),
            dst_ref=dst_ref.at[me],
            send_sem=send_sem.at[p],
            recv_sem=recv_sem.at[me],
            device_id=(c, p),
            device_id_type=MESH,
        ).wait_send()
        pltpu.make_async_remote_copy(
            src_ref=chunk(p),
            dst_ref=dst_ref.at[p],
            send_sem=send_sem.at[p],
            recv_sem=recv_sem.at[p],
            device_id=(c, p),
            device_id_type=MESH,
        ).wait_recv()
        return carry

    lax.fori_loop(1, n_ep, finish, 0)
    local.wait()


def exchange(src, per_peer, collective_id):
    n_ep = lax.axis_size("ep")
    block = src.shape[1:]
    moved = n_ep * math.prod(block) * src.dtype.itemsize
    return pl.pallas_call(
        functools.partial(exchange_kernel, per_peer),
        out_shape=jax.ShapeDtypeStruct((n_ep,) + block, src.dtype),
        in_specs=[pl.BlockSpec(memory_space=pl.ANY)],
        out_specs=pl.BlockSpec(memory_space=pl.ANY),
        scratch_shapes=[
            pltpu.SemaphoreType.DMA((n_ep,)),
            pltpu.SemaphoreType.DMA((n_ep,)),
            pltpu.SemaphoreType.DMA,
        ],
        compiler_params=pltpu.CompilerParams(
            collective_id=collective_id, has_side_effects=True
        ),
        cost_estimate=pl.CostEstimate(flops=0, transcendentals=0, bytes_accessed=2 * moved),
    )(src)


def run_expert(inputs, weight_in, weight_out, hidden_units):
    flat_in = inputs.reshape(-1, inputs.shape[-1])
    gate_up = jnp.dot(flat_in, weight_in, preferred_element_type=jnp.float32)
    activated = (jax.nn.silu(gate_up[:, :hidden_units]) * gate_up[:, hidden_units:]).astype(
        jnp.bfloat16
    )
    replies = jnp.dot(activated, weight_out, preferred_element_type=jnp.float32).astype(
        jnp.bfloat16
    )
    return replies.reshape(inputs.shape[:-1] + (weight_out.shape[-1],))


def shards(
    queries,
    keys,
    values,
    prior_out,
    prior_lse,
    residual,
    out_proj,
    norm_gain,
    expert_in,
    expert_out,
    expert_ids,
    route_weight,
):
    local_rows = queries.shape[0]
    ctx_count = lax.axis_size("ctx")
    ctx_here = lax.axis_index("ctx")
    ep_count = lax.axis_size("ep")
    reach_steps = min(2, ctx_count - 1)
    kv_pair = jnp.stack([keys, values])
    arrived = []
    current = kv_pair
    for stride in range(reach_steps):
        current = passed_along(current, "ctx", 1)
        arrived.append(current)
    window = jnp.concatenate(arrived, axis=1)
    width_kv = window.shape[1]
    key_win = window[0].reshape(width_kv, KVH, HD)
    value_win = window[1].reshape(width_kv, KVH, HD)
    query_blk = queries.reshape(local_rows, KVH, GROUP, HD)
    scores = jnp.einsum(
        "ighd,jgd->ghij", query_blk, key_win, preferred_element_type=jnp.float32
    ) / math.sqrt(HD)
    positions = jnp.arange(width_kv, dtype=jnp.int32)
    key_local = positions % local_rows
    key_ctx = (ctx_here - (positions // local_rows + 1)) % ctx_count
    query_local = jnp.arange(local_rows, dtype=jnp.int32)[:, None]
    visible = (key_local[None, :] < query_local) | (key_local[None, :] == query_local) & (
        key_ctx[None, :] <= ctx_here
    )
    scores = jnp.where(visible, scores, -jnp.inf)
    lse_prior = prior_lse.reshape(local_rows, KVH, GROUP).transpose(1, 2, 0)
    top_score = jnp.maximum(lse_prior, jnp.max(scores, axis=-1))
    weights = jnp.exp(scores - top_score[..., None])
    prior_weight = jnp.exp(lse_prior - top_score)
    totals = prior_weight + jnp.sum(weights, axis=-1)
    gathered = jnp.einsum(
        "ghij,jgd->ighd",
        weights.astype(jnp.bfloat16),
        value_win,
        preferred_element_type=jnp.float32,
    )
    prior_part = (
        prior_out.reshape(local_rows, KVH, GROUP, HD).astype(jnp.float32)
        * prior_weight.transpose(2, 0, 1)[..., None]
    )
    attended = ((prior_part + gathered) / totals.transpose(2, 0, 1)[..., None]).astype(jnp.bfloat16)
    attended = attended.reshape(local_rows, HEADS * HD)
    model_width = out_proj.shape[1]
    column_half = model_width // 2
    core = ctx_here % 2
    column_rows = lax.all_gather(out_proj, "ctx", axis=0, tiled=True)
    own_half = lax.dynamic_slice_in_dim(column_rows, core * column_half, column_half, axis=1)
    own_half = exchange(own_half[None], False, 0).reshape(-1, column_half)
    other_half = lax.ppermute(own_half, "ctx", [(i, i ^ 1) for i in range(ctx_count)])
    block_rows = out_proj.shape[0]
    attended_perm = (
        attended.reshape(local_rows, ctx_count, ep_count, block_rows)
        .transpose(0, 2, 1, 3)
        .reshape(local_rows, HEADS * HD)
    )
    own_part = jnp.dot(attended_perm, own_half, preferred_element_type=jnp.float32)
    other_part = jnp.dot(attended_perm, other_half, preferred_element_type=jnp.float32)
    projected = jnp.zeros((local_rows, model_width), jnp.float32)
    projected = lax.dynamic_update_slice_in_dim(projected, own_part, core * column_half, axis=1)
    projected = lax.dynamic_update_slice_in_dim(
        projected, other_part, (1 - core) * column_half, axis=1
    )
    mixed_state = (residual.astype(jnp.float32) + projected).astype(jnp.bfloat16)
    state_f = lax.optimization_barrier(mixed_state).astype(jnp.float32)
    normed = (
        state_f * lax.rsqrt(jnp.mean(state_f * state_f, axis=-1, keepdims=True) + 1e-06) * norm_gain
    ).astype(jnp.bfloat16)
    experts_all = ep_count * expert_in.shape[0]
    top_count = expert_ids.shape[1]
    capacity = max(
        local_rows // 4, top_count * ((local_rows + experts_all - 2) // (experts_all - 1))
    )
    flat_ids = expert_ids.reshape(-1)
    picks = flat_ids.shape[0]
    one_hot = (flat_ids[:, None] == jnp.arange(experts_all, dtype=jnp.int32)[None, :]).astype(
        jnp.bfloat16
    )
    pick_pos = jnp.arange(picks, dtype=jnp.int32)
    before = (pick_pos[None, :] < pick_pos[:, None]).astype(jnp.bfloat16)
    earlier = jnp.dot(before, one_hot, preferred_element_type=jnp.float32)
    rank = jnp.sum(earlier * one_hot.astype(jnp.float32), axis=1).astype(jnp.int32)
    slot_ids = (flat_ids * capacity + rank).reshape(local_rows, top_count)
    slot_pos = jnp.arange(experts_all * capacity, dtype=jnp.int32)
    take = jnp.any(slot_ids[None, :, :] == slot_pos[:, None, None], axis=2).astype(jnp.bfloat16)
    outgoing = (
        jnp.dot(take, normed, preferred_element_type=jnp.float32)
        .astype(jnp.bfloat16)
        .reshape(experts_all, capacity, model_width)
    )
    weight_in = expert_in[0]
    weight_out = expert_out[0]
    hidden_units = weight_out.shape[0]
    replies = run_expert(
        exchange(outgoing, True, 1),
        weight_in,
        weight_out,
        hidden_units,
    )
    returned = exchange(replies, True, 2)
    spread = jnp.sum(
        jnp.where(
            slot_ids[:, :, None] == slot_pos[None, None, :], route_weight[:, :, None], 0.0
        ),
        axis=1,
    )
    combined = jnp.dot(
        spread,
        returned.reshape(experts_all * capacity, model_width).astype(jnp.float32),
        precision=lax.Precision.HIGHEST,
        preferred_element_type=jnp.float32,
    )
    layer_out = (state_f + combined).astype(jnp.bfloat16)
    return (layer_out, attended)


def solution(mesh):
    return jax.shard_map(
        shards,
        mesh=mesh,
        in_specs=(
            P(("ctx", "ep"), None),
            P(("ctx", "ep"), None),
            P(("ctx", "ep"), None),
            P(("ctx", "ep"), None),
            P(("ctx", "ep"), None),
            P(("ctx", "ep"), None),
            P(("ctx", "ep"), None),
            P(),
            P("ep", None, None),
            P("ep", None, None),
            P(("ctx", "ep"), None),
            P(("ctx", "ep"), None),
        ),
        out_specs=(P(("ctx", "ep"), None), P(("ctx", "ep"), None)),
        check_vma=False,
    )
```

```python
import functools
import math

import jax
import jax.numpy as jnp
from jax import lax
from jax.experimental import pallas as pl
from jax.experimental.pallas import tpu as pltpu
from jax.sharding import PartitionSpec as P

MESH = pl.DeviceIdType.MESH

HEADS = 16
KVH = 2
HD = 128
GROUP = 8


def passed_along(shard, axis, by):
    devices = lax.axis_size(axis)
    return lax.ppermute(shard, axis, [(i, (i + by) % devices) for i in range(devices)])


def exchange_kernel(per_peer, src_ref, dst_ref, send_sem, recv_sem, local_sem):
    n_ep = lax.axis_size("ep")
    n_ctx = lax.axis_size("ctx")
    me = lax.axis_index("ep")
    ctx_me = lax.axis_index("ctx")
    ctx_far = (ctx_me + n_ctx // 2) % n_ctx

    core = ctx_me % 2

    bits = max(n_ep - 1, 1).bit_length()

    def peer(j):
        step = j + core * (n_ep - 2 * j)
        p = 0
        for b in range(bits):
            p = p + ((me // 2**b + step // 2**b) % 2) * 2**b
        same = 1 - (p + me) % 2
        return p, same * ctx_me + (1 - same) * ctx_far

    def chunk(p):
        return src_ref.at[p] if per_peer else src_ref.at[0]

    barrier = pltpu.get_barrier_semaphore()

    def greet(j, carry):
        p, c = peer(j)
        pl.semaphore_signal(barrier, inc=1, device_id=(c, p), device_id_type=MESH)
        return carry

    lax.fori_loop(1, n_ep, greet, 0)
    pl.semaphore_wait(barrier, n_ep - 1)

    local = pltpu.make_async_copy(chunk(me), dst_ref.at[me], local_sem)
    local.start()

    def send(j, carry):
        p, c = peer(j)
        pltpu.make_async_remote_copy(
            src_ref=chunk(p),
            dst_ref=dst_ref.at[me],
            send_sem=send_sem.at[p],
            recv_sem=recv_sem.at[me],
            device_id=(c, p),
            device_id_type=MESH,
        ).start()
        return carry

    lax.fori_loop(1, n_ep, send, 0)

    def finish(j, carry):
        p, c = peer(j)
        pltpu.make_async_remote_copy(
            src_ref=chunk(p),
            dst_ref=dst_ref.at[me],
            send_sem=send_sem.at[p],
            recv_sem=recv_sem.at[me],
            device_id=(c, p),
            device_id_type=MESH,
        ).wait_send()
        pltpu.make_async_remote_copy(
            src_ref=chunk(p),
            dst_ref=dst_ref.at[p],
            send_sem=send_sem.at[p],
            recv_sem=recv_sem.at[p],
            device_id=(c, p),
            device_id_type=MESH,
        ).wait_recv()
        return carry

    lax.fori_loop(1, n_ep, finish, 0)
    local.wait()


def exchange(src, per_peer, collective_id):
    n_ep = lax.axis_size("ep")
    block = src.shape[1:]
    moved = n_ep * math.prod(block) * src.dtype.itemsize
    return pl.pallas_call(
        functools.partial(exchange_kernel, per_peer),
        out_shape=jax.ShapeDtypeStruct((n_ep,) + block, src.dtype),
        in_specs=[pl.BlockSpec(memory_space=pl.ANY)],
        out_specs=pl.BlockSpec(memory_space=pl.ANY),
        scratch_shapes=[
            pltpu.SemaphoreType.DMA((n_ep,)),
            pltpu.SemaphoreType.DMA((n_ep,)),
            pltpu.SemaphoreType.DMA,
        ],
        compiler_params=pltpu.CompilerParams(
            collective_id=collective_id, has_side_effects=True
        ),
        cost_estimate=pl.CostEstimate(flops=0, transcendentals=0, bytes_accessed=2 * moved),
    )(src)


def run_expert(inputs, weight_in, weight_out, hidden_units):
    flat_in = inputs.reshape(-1, inputs.shape[-1])
    gate_up = jnp.dot(flat_in, weight_in, preferred_element_type=jnp.float32)
    activated = (jax.nn.silu(gate_up[:, :hidden_units]) * gate_up[:, hidden_units:]).astype(
        jnp.bfloat16
    )
    replies = jnp.dot(activated, weight_out, preferred_element_type=jnp.float32).astype(
        jnp.bfloat16
    )
    return replies.reshape(inputs.shape[:-1] + (weight_out.shape[-1],))


def shards(
    queries,
    keys,
    values,
    prior_out,
    prior_lse,
    residual,
    out_proj,
    norm_gain,
    expert_in,
    expert_out,
    expert_ids,
    route_weight,
):
    local_rows = queries.shape[0]
    ctx_count = lax.axis_size("ctx")
    ctx_here = lax.axis_index("ctx")
    ep_count = lax.axis_size("ep")
    reach_steps = min(2, ctx_count - 1)
    kv_pair = jnp.stack([keys, values])
    arrived = []
    current = kv_pair
    for stride in range(reach_steps):
        current = passed_along(current, "ctx", 1)
        arrived.append(current)
    window = jnp.concatenate(arrived, axis=1)
    width_kv = window.shape[1]
    key_win = window[0].reshape(width_kv, KVH, HD)
    value_win = window[1].reshape(width_kv, KVH, HD)
    query_blk = queries.reshape(local_rows, KVH, GROUP, HD)
    scores = jnp.einsum(
        "ighd,jgd->ghij", query_blk, key_win, preferred_element_type=jnp.float32
    ) / math.sqrt(HD)
    positions = jnp.arange(width_kv, dtype=jnp.int32)
    key_local = positions % local_rows
    key_ctx = (ctx_here - (positions // local_rows + 1)) % ctx_count
    query_local = jnp.arange(local_rows, dtype=jnp.int32)[:, None]
    visible = (key_local[None, :] < query_local) | (key_local[None, :] == query_local) & (
        key_ctx[None, :] <= ctx_here
    )
    scores = jnp.where(visible, scores, -jnp.inf)
    lse_prior = prior_lse.reshape(local_rows, KVH, GROUP).transpose(1, 2, 0)
    top_score = jnp.maximum(lse_prior, jnp.max(scores, axis=-1))
    weights = jnp.exp(scores - top_score[..., None])
    prior_weight = jnp.exp(lse_prior - top_score)
    totals = prior_weight + jnp.sum(weights, axis=-1)
    gathered = jnp.einsum(
        "ghij,jgd->ighd",
        weights.astype(jnp.bfloat16),
        value_win,
        preferred_element_type=jnp.float32,
    )
    prior_part = (
        prior_out.reshape(local_rows, KVH, GROUP, HD).astype(jnp.float32)
        * prior_weight.transpose(2, 0, 1)[..., None]
    )
    attended = ((prior_part + gathered) / totals.transpose(2, 0, 1)[..., None]).astype(jnp.bfloat16)
    attended = attended.reshape(local_rows, HEADS * HD)
    model_width = out_proj.shape[1]
    column_half = model_width // 2
    core = ctx_here % 2
    block_count = out_proj.shape[0]
    column_rows = jnp.zeros((ctx_count * block_count, model_width), out_proj.dtype)
    column_rows = lax.dynamic_update_slice_in_dim(
        column_rows, out_proj, ctx_here * block_count, axis=0
    )
    for shift in range(1, ctx_count):
        arrived_block = passed_along(out_proj, "ctx", shift)
        column_rows = lax.dynamic_update_slice_in_dim(
            column_rows, arrived_block, ((ctx_here - shift) % ctx_count) * block_count, axis=0
        )
    own_half = lax.dynamic_slice_in_dim(column_rows, core * column_half, column_half, axis=1)
    own_half = exchange(own_half[None], False, 0).reshape(-1, column_half)
    other_half = lax.ppermute(own_half, "ctx", [(i, i ^ 1) for i in range(ctx_count)])
    block_rows = out_proj.shape[0]
    attended_perm = (
        attended.reshape(local_rows, ctx_count, ep_count, block_rows)
        .transpose(0, 2, 1, 3)
        .reshape(local_rows, HEADS * HD)
    )
    own_part = jnp.dot(attended_perm, own_half, preferred_element_type=jnp.float32)
    other_part = jnp.dot(attended_perm, other_half, preferred_element_type=jnp.float32)
    projected = jnp.zeros((local_rows, model_width), jnp.float32)
    projected = lax.dynamic_update_slice_in_dim(projected, own_part, core * column_half, axis=1)
    projected = lax.dynamic_update_slice_in_dim(
        projected, other_part, (1 - core) * column_half, axis=1
    )
    mixed_state = (residual.astype(jnp.float32) + projected).astype(jnp.bfloat16)
    state_f = lax.optimization_barrier(mixed_state).astype(jnp.float32)
    normed = (
        state_f * lax.rsqrt(jnp.mean(state_f * state_f, axis=-1, keepdims=True) + 1e-06) * norm_gain
    ).astype(jnp.bfloat16)
    experts_all = ep_count * expert_in.shape[0]
    top_count = expert_ids.shape[1]
    capacity = max(
        local_rows // 4, top_count * ((local_rows + experts_all - 2) // (experts_all - 1))
    )
    flat_ids = expert_ids.reshape(-1)
    picks = flat_ids.shape[0]
    one_hot = (flat_ids[:, None] == jnp.arange(experts_all, dtype=jnp.int32)[None, :]).astype(
        jnp.bfloat16
    )
    pick_pos = jnp.arange(picks, dtype=jnp.int32)
    before = (pick_pos[None, :] < pick_pos[:, None]).astype(jnp.bfloat16)
    earlier = jnp.dot(before, one_hot, preferred_element_type=jnp.float32)
    rank = jnp.sum(earlier * one_hot.astype(jnp.float32), axis=1).astype(jnp.int32)
    slot_ids = (flat_ids * capacity + rank).reshape(local_rows, top_count)
    slot_pos = jnp.arange(experts_all * capacity, dtype=jnp.int32)
    take = jnp.any(slot_ids[None, :, :] == slot_pos[:, None, None], axis=2).astype(jnp.bfloat16)
    outgoing = (
        jnp.dot(take, normed, preferred_element_type=jnp.float32)
        .astype(jnp.bfloat16)
        .reshape(experts_all, capacity, model_width)
    )
    weight_in = expert_in[0]
    weight_out = expert_out[0]
    hidden_units = weight_out.shape[0]
    replies = run_expert(
        exchange(outgoing, True, 1),
        weight_in,
        weight_out,
        hidden_units,
    )
    returned = exchange(replies, True, 2)
    spread = jnp.sum(
        jnp.where(
            slot_ids[:, :, None] == slot_pos[None, None, :], route_weight[:, :, None], 0.0
        ),
        axis=1,
    )
    combined = jnp.dot(
        spread,
        returned.reshape(experts_all * capacity, model_width).astype(jnp.float32),
        precision=lax.Precision.HIGHEST,
        preferred_element_type=jnp.float32,
    )
    layer_out = (state_f + combined).astype(jnp.bfloat16)
    return (layer_out, attended)


def solution(mesh):
    return jax.shard_map(
        shards,
        mesh=mesh,
        in_specs=(
            P(("ctx", "ep"), None),
            P(("ctx", "ep"), None),
            P(("ctx", "ep"), None),
            P(("ctx", "ep"), None),
            P(("ctx", "ep"), None),
            P(("ctx", "ep"), None),
            P(("ctx", "ep"), None),
            P(),
            P("ep", None, None),
            P("ep", None, None),
            P(("ctx", "ep"), None),
            P(("ctx", "ep"), None),
        ),
        out_specs=(P(("ctx", "ep"), None), P(("ctx", "ep"), None)),
        check_vma=False,
    )
```

```python
import functools
import math

import jax
import jax.numpy as jnp
from jax import lax
from jax.experimental import pallas as pl
from jax.experimental.pallas import tpu as pltpu
from jax.sharding import PartitionSpec as P

MESH = pl.DeviceIdType.MESH

HEADS = 16
KVH = 2
HD = 128
GROUP = 8


def passed_along(shard, axis, by):
    devices = lax.axis_size(axis)
    return lax.ppermute(shard, axis, [(i, (i + by) % devices) for i in range(devices)])


def exchange_kernel(per_peer, src_ref, dst_ref, send_sem, recv_sem, local_sem):
    n_ep = lax.axis_size("ep")
    n_ctx = lax.axis_size("ctx")
    me = lax.axis_index("ep")
    ctx_me = lax.axis_index("ctx")
    ctx_far = (ctx_me + n_ctx // 2) % n_ctx

    core = ctx_me % 2

    bits = max(n_ep - 1, 1).bit_length()

    def peer(j):
        step = j + core * (n_ep - 2 * j)
        p = 0
        for b in range(bits):
            p = p + ((me // 2**b + step // 2**b) % 2) * 2**b
        same = 1 - (p + me) % 2
        return p, same * ctx_me + (1 - same) * ctx_far

    def chunk(p):
        return src_ref.at[p] if per_peer else src_ref.at[0]

    barrier = pltpu.get_barrier_semaphore()

    def greet(j, carry):
        p, c = peer(j)
        pl.semaphore_signal(barrier, inc=1, device_id=(c, p), device_id_type=MESH)
        return carry

    lax.fori_loop(1, n_ep, greet, 0)
    pl.semaphore_wait(barrier, n_ep - 1)

    local = pltpu.make_async_copy(chunk(me), dst_ref.at[me], local_sem)
    local.start()

    def send(j, carry):
        p, c = peer(j)
        pltpu.make_async_remote_copy(
            src_ref=chunk(p),
            dst_ref=dst_ref.at[me],
            send_sem=send_sem.at[p],
            recv_sem=recv_sem.at[me],
            device_id=(c, p),
            device_id_type=MESH,
        ).start()
        return carry

    lax.fori_loop(1, n_ep, send, 0)

    def finish(j, carry):
        p, c = peer(j)
        pltpu.make_async_remote_copy(
            src_ref=chunk(p),
            dst_ref=dst_ref.at[me],
            send_sem=send_sem.at[p],
            recv_sem=recv_sem.at[me],
            device_id=(c, p),
            device_id_type=MESH,
        ).wait_send()
        pltpu.make_async_remote_copy(
            src_ref=chunk(p),
            dst_ref=dst_ref.at[p],
            send_sem=send_sem.at[p],
            recv_sem=recv_sem.at[p],
            device_id=(c, p),
            device_id_type=MESH,
        ).wait_recv()
        return carry

    lax.fori_loop(1, n_ep, finish, 0)
    local.wait()


def exchange(src, per_peer, collective_id):
    n_ep = lax.axis_size("ep")
    block = src.shape[1:]
    moved = n_ep * math.prod(block) * src.dtype.itemsize
    return pl.pallas_call(
        functools.partial(exchange_kernel, per_peer),
        out_shape=jax.ShapeDtypeStruct((n_ep,) + block, src.dtype),
        in_specs=[pl.BlockSpec(memory_space=pl.ANY)],
        out_specs=pl.BlockSpec(memory_space=pl.ANY),
        scratch_shapes=[
            pltpu.SemaphoreType.DMA((n_ep,)),
            pltpu.SemaphoreType.DMA((n_ep,)),
            pltpu.SemaphoreType.DMA,
        ],
        compiler_params=pltpu.CompilerParams(
            collective_id=collective_id, has_side_effects=True
        ),
        cost_estimate=pl.CostEstimate(flops=0, transcendentals=0, bytes_accessed=2 * moved),
    )(src)


def run_expert(inputs, weight_in, weight_out, hidden_units):
    flat_in = inputs.reshape(-1, inputs.shape[-1])
    gate_up = jnp.dot(flat_in, weight_in, preferred_element_type=jnp.float32)
    activated = (jax.nn.silu(gate_up[:, :hidden_units]) * gate_up[:, hidden_units:]).astype(
        jnp.bfloat16
    )
    replies = jnp.dot(activated, weight_out, preferred_element_type=jnp.float32).astype(
        jnp.bfloat16
    )
    return replies.reshape(inputs.shape[:-1] + (weight_out.shape[-1],))


def shards(
    queries,
    keys,
    values,
    prior_out,
    prior_lse,
    residual,
    out_proj,
    norm_gain,
    expert_in,
    expert_out,
    expert_ids,
    route_weight,
):
    local_rows = queries.shape[0]
    ctx_count = lax.axis_size("ctx")
    ctx_here = lax.axis_index("ctx")
    ep_count = lax.axis_size("ep")
    reach_steps = min(2, ctx_count - 1)
    kv_pair = jnp.stack([keys, values])
    arrived = []
    current = kv_pair
    for stride in range(reach_steps):
        current = passed_along(current, "ctx", 1)
        arrived.append(current)
    window = jnp.concatenate(arrived, axis=1)
    width_kv = window.shape[1]
    key_win = window[0].reshape(width_kv, KVH, HD)
    value_win = window[1].reshape(width_kv, KVH, HD)
    query_blk = queries.reshape(local_rows, KVH, GROUP, HD)
    scores = jnp.einsum(
        "ighd,jgd->ghij", query_blk, key_win, preferred_element_type=jnp.float32
    ) / math.sqrt(HD)
    positions = jnp.arange(width_kv, dtype=jnp.int32)
    key_local = positions % local_rows
    key_ctx = (ctx_here - (positions // local_rows + 1)) % ctx_count
    query_local = jnp.arange(local_rows, dtype=jnp.int32)[:, None]
    visible = (key_local[None, :] < query_local) | (key_local[None, :] == query_local) & (
        key_ctx[None, :] <= ctx_here
    )
    scores = jnp.where(visible, scores, -jnp.inf)
    lse_prior = prior_lse.reshape(local_rows, KVH, GROUP).transpose(1, 2, 0)
    top_score = jnp.maximum(lse_prior, jnp.max(scores, axis=-1))
    weights = jnp.exp(scores - top_score[..., None])
    prior_weight = jnp.exp(lse_prior - top_score)
    totals = prior_weight + jnp.sum(weights, axis=-1)
    gathered = jnp.einsum(
        "ghij,jgd->ighd",
        weights.astype(jnp.bfloat16),
        value_win,
        preferred_element_type=jnp.float32,
    )
    prior_part = (
        prior_out.reshape(local_rows, KVH, GROUP, HD).astype(jnp.float32)
        * prior_weight.transpose(2, 0, 1)[..., None]
    )
    attended = ((prior_part + gathered) / totals.transpose(2, 0, 1)[..., None]).astype(jnp.bfloat16)
    attended = attended.reshape(local_rows, HEADS * HD)
    model_width = out_proj.shape[1]
    column_half = model_width // 2
    core = ctx_here % 2
    block_count = out_proj.shape[0]
    column_rows = jnp.zeros((ctx_count * block_count, model_width), out_proj.dtype)
    column_rows = lax.dynamic_update_slice_in_dim(
        column_rows, out_proj, ctx_here * block_count, axis=0
    )
    for shift in range(1, ctx_count):
        arrived_block = passed_along(out_proj, "ctx", shift)
        column_rows = lax.dynamic_update_slice_in_dim(
            column_rows, arrived_block, ((ctx_here - shift) % ctx_count) * block_count, axis=0
        )
    own_half = lax.dynamic_slice_in_dim(column_rows, core * column_half, column_half, axis=1)
    own_half, attended = lax.optimization_barrier((own_half, attended))
    own_half = exchange(own_half[None], False, 0).reshape(-1, column_half)
    other_half = lax.ppermute(own_half, "ctx", [(i, i ^ 1) for i in range(ctx_count)])
    block_rows = out_proj.shape[0]
    attended_perm = (
        attended.reshape(local_rows, ctx_count, ep_count, block_rows)
        .transpose(0, 2, 1, 3)
        .reshape(local_rows, HEADS * HD)
    )
    own_part = jnp.dot(attended_perm, own_half, preferred_element_type=jnp.float32)
    other_part = jnp.dot(attended_perm, other_half, preferred_element_type=jnp.float32)
    projected = jnp.zeros((local_rows, model_width), jnp.float32)
    projected = lax.dynamic_update_slice_in_dim(projected, own_part, core * column_half, axis=1)
    projected = lax.dynamic_update_slice_in_dim(
        projected, other_part, (1 - core) * column_half, axis=1
    )
    mixed_state = (residual.astype(jnp.float32) + projected).astype(jnp.bfloat16)
    state_f = lax.optimization_barrier(mixed_state).astype(jnp.float32)
    normed = (
        state_f * lax.rsqrt(jnp.mean(state_f * state_f, axis=-1, keepdims=True) + 1e-06) * norm_gain
    ).astype(jnp.bfloat16)
    experts_all = ep_count * expert_in.shape[0]
    top_count = expert_ids.shape[1]
    capacity = max(
        local_rows // 4, top_count * ((local_rows + experts_all - 2) // (experts_all - 1))
    )
    flat_ids = expert_ids.reshape(-1)
    picks = flat_ids.shape[0]
    one_hot = (flat_ids[:, None] == jnp.arange(experts_all, dtype=jnp.int32)[None, :]).astype(
        jnp.bfloat16
    )
    pick_pos = jnp.arange(picks, dtype=jnp.int32)
    before = (pick_pos[None, :] < pick_pos[:, None]).astype(jnp.bfloat16)
    earlier = jnp.dot(before, one_hot, preferred_element_type=jnp.float32)
    rank = jnp.sum(earlier * one_hot.astype(jnp.float32), axis=1).astype(jnp.int32)
    slot_ids = (flat_ids * capacity + rank).reshape(local_rows, top_count)
    slot_pos = jnp.arange(experts_all * capacity, dtype=jnp.int32)
    take = jnp.any(slot_ids[None, :, :] == slot_pos[:, None, None], axis=2).astype(jnp.bfloat16)
    outgoing = (
        jnp.dot(take, normed, preferred_element_type=jnp.float32)
        .astype(jnp.bfloat16)
        .reshape(experts_all, capacity, model_width)
    )
    weight_in = expert_in[0]
    weight_out = expert_out[0]
    hidden_units = weight_out.shape[0]
    replies = run_expert(
        exchange(outgoing, True, 1),
        weight_in,
        weight_out,
        hidden_units,
    )
    returned = exchange(replies, True, 2)
    spread = jnp.sum(
        jnp.where(
            slot_ids[:, :, None] == slot_pos[None, None, :], route_weight[:, :, None], 0.0
        ),
        axis=1,
    )
    combined = jnp.dot(
        spread,
        returned.reshape(experts_all * capacity, model_width).astype(jnp.float32),
        precision=lax.Precision.HIGHEST,
        preferred_element_type=jnp.float32,
    )
    layer_out = (state_f + combined).astype(jnp.bfloat16)
    return (layer_out, attended)


def solution(mesh):
    return jax.shard_map(
        shards,
        mesh=mesh,
        in_specs=(
            P(("ctx", "ep"), None),
            P(("ctx", "ep"), None),
            P(("ctx", "ep"), None),
            P(("ctx", "ep"), None),
            P(("ctx", "ep"), None),
            P(("ctx", "ep"), None),
            P(("ctx", "ep"), None),
            P(),
            P("ep", None, None),
            P("ep", None, None),
            P(("ctx", "ep"), None),
            P(("ctx", "ep"), None),
        ),
        out_specs=(P(("ctx", "ep"), None), P(("ctx", "ep"), None)),
        check_vma=False,
    )
```

```python
import functools
import math

import jax
import jax.numpy as jnp
from jax import lax
from jax.experimental import pallas as pl
from jax.experimental.pallas import tpu as pltpu
from jax.sharding import PartitionSpec as P

MESH = pl.DeviceIdType.MESH

HEADS = 16
KVH = 2
HD = 128
GROUP = 8


def passed_along(shard, axis, by):
    devices = lax.axis_size(axis)
    return lax.ppermute(shard, axis, [(i, (i + by) % devices) for i in range(devices)])


def exchange_kernel(per_peer, src_ref, dst_ref, send_sem, recv_sem, local_sem):
    n_ep = lax.axis_size("ep")
    n_ctx = lax.axis_size("ctx")
    me = lax.axis_index("ep")
    ctx_me = lax.axis_index("ctx")
    ctx_far = (ctx_me + n_ctx // 2) % n_ctx

    core = ctx_me % 2

    bits = max(n_ep - 1, 1).bit_length()

    def peer(j):
        step = j + core * (n_ep - 2 * j)
        p = 0
        for b in range(bits):
            p = p + ((me // 2**b + step // 2**b) % 2) * 2**b
        same = 1 - (p + me) % 2
        return p, same * ctx_me + (1 - same) * ctx_far

    def chunk(p):
        return src_ref.at[p] if per_peer else src_ref.at[0]

    barrier = pltpu.get_barrier_semaphore()

    def greet(j, carry):
        p, c = peer(j)
        pl.semaphore_signal(barrier, inc=1, device_id=(c, p), device_id_type=MESH)
        return carry

    lax.fori_loop(1, n_ep, greet, 0)
    pl.semaphore_wait(barrier, n_ep - 1)

    local = pltpu.make_async_copy(chunk(me), dst_ref.at[me], local_sem)
    local.start()

    def send(j, carry):
        p, c = peer(j)
        pltpu.make_async_remote_copy(
            src_ref=chunk(p),
            dst_ref=dst_ref.at[me],
            send_sem=send_sem.at[p],
            recv_sem=recv_sem.at[me],
            device_id=(c, p),
            device_id_type=MESH,
        ).start()
        return carry

    lax.fori_loop(1, n_ep, send, 0)

    def finish(j, carry):
        p, c = peer(j)
        pltpu.make_async_remote_copy(
            src_ref=chunk(p),
            dst_ref=dst_ref.at[me],
            send_sem=send_sem.at[p],
            recv_sem=recv_sem.at[me],
            device_id=(c, p),
            device_id_type=MESH,
        ).wait_send()
        pltpu.make_async_remote_copy(
            src_ref=chunk(p),
            dst_ref=dst_ref.at[p],
            send_sem=send_sem.at[p],
            recv_sem=recv_sem.at[p],
            device_id=(c, p),
            device_id_type=MESH,
        ).wait_recv()
        return carry

    lax.fori_loop(1, n_ep, finish, 0)
    local.wait()


def exchange(src, per_peer, collective_id):
    n_ep = lax.axis_size("ep")
    block = src.shape[1:]
    moved = n_ep * math.prod(block) * src.dtype.itemsize
    return pl.pallas_call(
        functools.partial(exchange_kernel, per_peer),
        out_shape=jax.ShapeDtypeStruct((n_ep,) + block, src.dtype),
        in_specs=[pl.BlockSpec(memory_space=pl.ANY)],
        out_specs=pl.BlockSpec(memory_space=pl.ANY),
        scratch_shapes=[
            pltpu.SemaphoreType.DMA((n_ep,)),
            pltpu.SemaphoreType.DMA((n_ep,)),
            pltpu.SemaphoreType.DMA,
        ],
        compiler_params=pltpu.CompilerParams(
            collective_id=collective_id, has_side_effects=True
        ),
        cost_estimate=pl.CostEstimate(flops=0, transcendentals=0, bytes_accessed=2 * moved),
    )(src)


def run_expert(inputs, weight_in, weight_out, hidden_units):
    flat_in = inputs.reshape(-1, inputs.shape[-1])
    gate_up = jnp.dot(flat_in, weight_in, preferred_element_type=jnp.float32)
    activated = (jax.nn.silu(gate_up[:, :hidden_units]) * gate_up[:, hidden_units:]).astype(
        jnp.bfloat16
    )
    replies = jnp.dot(activated, weight_out, preferred_element_type=jnp.float32).astype(
        jnp.bfloat16
    )
    return replies.reshape(inputs.shape[:-1] + (weight_out.shape[-1],))


def shards(
    queries,
    keys,
    values,
    prior_out,
    prior_lse,
    residual,
    out_proj,
    norm_gain,
    expert_in,
    expert_out,
    expert_ids,
    route_weight,
):
    local_rows = queries.shape[0]
    ctx_count = lax.axis_size("ctx")
    ctx_here = lax.axis_index("ctx")
    ep_count = lax.axis_size("ep")
    reach_steps = min(2, ctx_count - 1)
    kv_pair = jnp.stack([keys, values])
    arrived = []
    current = kv_pair
    for stride in range(reach_steps):
        current = passed_along(current, "ctx", 1)
        arrived.append(current)
    window = jnp.concatenate(arrived, axis=1)
    width_kv = window.shape[1]
    key_win = window[0].reshape(width_kv, KVH, HD)
    value_win = window[1].reshape(width_kv, KVH, HD)
    query_blk = queries.reshape(local_rows, KVH, GROUP, HD)
    scores = jnp.einsum(
        "ighd,jgd->ghij", query_blk, key_win, preferred_element_type=jnp.float32
    ) / math.sqrt(HD)
    positions = jnp.arange(width_kv, dtype=jnp.int32)
    key_local = positions % local_rows
    key_ctx = (ctx_here - (positions // local_rows + 1)) % ctx_count
    query_local = jnp.arange(local_rows, dtype=jnp.int32)[:, None]
    visible = (key_local[None, :] < query_local) | (key_local[None, :] == query_local) & (
        key_ctx[None, :] <= ctx_here
    )
    scores = jnp.where(visible, scores, -jnp.inf)
    lse_prior = prior_lse.reshape(local_rows, KVH, GROUP).transpose(1, 2, 0)
    top_score = jnp.maximum(lse_prior, jnp.max(scores, axis=-1))
    weights = jnp.exp(scores - top_score[..., None])
    prior_weight = jnp.exp(lse_prior - top_score)
    totals = prior_weight + jnp.sum(weights, axis=-1)
    gathered = jnp.einsum(
        "ghij,jgd->ighd",
        weights.astype(jnp.bfloat16),
        value_win,
        preferred_element_type=jnp.float32,
    )
    prior_part = (
        prior_out.reshape(local_rows, KVH, GROUP, HD).astype(jnp.float32)
        * prior_weight.transpose(2, 0, 1)[..., None]
    )
    attended = ((prior_part + gathered) / totals.transpose(2, 0, 1)[..., None]).astype(jnp.bfloat16)
    attended = attended.reshape(local_rows, HEADS * HD)
    model_width = out_proj.shape[1]
    column_half = model_width // 2
    core = ctx_here % 2
    block_count = out_proj.shape[0]
    column_rows = jnp.zeros((ctx_count * block_count, model_width), out_proj.dtype)
    column_rows = lax.dynamic_update_slice_in_dim(
        column_rows, out_proj, ctx_here * block_count, axis=0
    )
    distance = 1
    while distance < ctx_count:
        partner = [(i, i ^ distance) for i in range(ctx_count)]
        column_rows = column_rows + lax.ppermute(column_rows, "ctx", partner)
        distance *= 2
    own_half = lax.dynamic_slice_in_dim(column_rows, core * column_half, column_half, axis=1)
    own_half = exchange(own_half[None], False, 0).reshape(-1, column_half)
    other_half = lax.ppermute(own_half, "ctx", [(i, i ^ 1) for i in range(ctx_count)])
    block_rows = out_proj.shape[0]
    attended_perm = (
        attended.reshape(local_rows, ctx_count, ep_count, block_rows)
        .transpose(0, 2, 1, 3)
        .reshape(local_rows, HEADS * HD)
    )
    own_part = jnp.dot(attended_perm, own_half, preferred_element_type=jnp.float32)
    other_part = jnp.dot(attended_perm, other_half, preferred_element_type=jnp.float32)
    projected = jnp.zeros((local_rows, model_width), jnp.float32)
    projected = lax.dynamic_update_slice_in_dim(projected, own_part, core * column_half, axis=1)
    projected = lax.dynamic_update_slice_in_dim(
        projected, other_part, (1 - core) * column_half, axis=1
    )
    mixed_state = (residual.astype(jnp.float32) + projected).astype(jnp.bfloat16)
    state_f = lax.optimization_barrier(mixed_state).astype(jnp.float32)
    normed = (
        state_f * lax.rsqrt(jnp.mean(state_f * state_f, axis=-1, keepdims=True) + 1e-06) * norm_gain
    ).astype(jnp.bfloat16)
    experts_all = ep_count * expert_in.shape[0]
    top_count = expert_ids.shape[1]
    capacity = max(
        local_rows // 4, top_count * ((local_rows + experts_all - 2) // (experts_all - 1))
    )
    flat_ids = expert_ids.reshape(-1)
    picks = flat_ids.shape[0]
    one_hot = (flat_ids[:, None] == jnp.arange(experts_all, dtype=jnp.int32)[None, :]).astype(
        jnp.bfloat16
    )
    pick_pos = jnp.arange(picks, dtype=jnp.int32)
    before = (pick_pos[None, :] < pick_pos[:, None]).astype(jnp.bfloat16)
    earlier = jnp.dot(before, one_hot, preferred_element_type=jnp.float32)
    rank = jnp.sum(earlier * one_hot.astype(jnp.float32), axis=1).astype(jnp.int32)
    slot_ids = (flat_ids * capacity + rank).reshape(local_rows, top_count)
    slot_pos = jnp.arange(experts_all * capacity, dtype=jnp.int32)
    take = jnp.any(slot_ids[None, :, :] == slot_pos[:, None, None], axis=2).astype(jnp.bfloat16)
    outgoing = (
        jnp.dot(take, normed, preferred_element_type=jnp.float32)
        .astype(jnp.bfloat16)
        .reshape(experts_all, capacity, model_width)
    )
    weight_in = expert_in[0]
    weight_out = expert_out[0]
    hidden_units = weight_out.shape[0]
    replies = run_expert(
        exchange(outgoing, True, 1),
        weight_in,
        weight_out,
        hidden_units,
    )
    returned = exchange(replies, True, 2)
    spread = jnp.sum(
        jnp.where(
            slot_ids[:, :, None] == slot_pos[None, None, :], route_weight[:, :, None], 0.0
        ),
        axis=1,
    )
    combined = jnp.dot(
        spread,
        returned.reshape(experts_all * capacity, model_width).astype(jnp.float32),
        precision=lax.Precision.HIGHEST,
        preferred_element_type=jnp.float32,
    )
    layer_out = (state_f + combined).astype(jnp.bfloat16)
    return (layer_out, attended)


def solution(mesh):
    return jax.shard_map(
        shards,
        mesh=mesh,
        in_specs=(
            P(("ctx", "ep"), None),
            P(("ctx", "ep"), None),
            P(("ctx", "ep"), None),
            P(("ctx", "ep"), None),
            P(("ctx", "ep"), None),
            P(("ctx", "ep"), None),
            P(("ctx", "ep"), None),
            P(),
            P("ep", None, None),
            P("ep", None, None),
            P(("ctx", "ep"), None),
            P(("ctx", "ep"), None),
        ),
        out_specs=(P(("ctx", "ep"), None), P(("ctx", "ep"), None)),
        check_vma=False,
    )
```
